256 devices in a mesh: section: 4 (over y), dp: 64 (over x, z, core).
Axes of the slice: x: 4, y: 4, z: 8, core: 2. Of those that a mesh axis runs over, the one named last changes fastest.
Arguments:
- hidden_in: bfloat16 [2, 4, 4, 1024, 4096], P(None, 'section', None, 'dp'), may hold values from -6 to 6
- out_grad: bfloat16 [4, 1024, 4096], P(None, 'dp'), may hold values from -6 to 6
- gate_probs: float32 [2, 4, 4, 1024, 2], P(None, 'section', None, 'dp'), may hold values from 0.1 to 1
- expert_ids: int32 [2, 4, 4, 1024, 2], P(None, 'section', None, 'dp'), may hold values from 0 to 7, all different within a row
- task_ids: int32 [4, 64], P(None, 'dp'), may hold values from 0 to 1
- task_embed: float32 [2, 256], replicated, may hold values from -5 to 5
- slot_embed: float32 [2, 4, 8, 256], P(None, 'section'), may hold values from -5 to 5
- gen_down: bfloat16 [256, 65536], P(None, 'dp'), may hold values from -0.0078125 to 0.0078125
- gen_up: bfloat16 [256, 65536], P(None, 'dp'), may hold values from -0.09375 to 0.09375
Outputs:
- d_hidden: bfloat16 [4, 4, 1024, 4096], P('section', None, 'dp')
- d_gen_down: float32 [256, 65536], P(None, 'dp')
- d_gen_up: float32 [256, 65536], P(None, 'dp')
- d_task_embed: float32 [2, 256], replicated
- d_slot_embed: float32 [2, 4, 8, 256], P(None, 'section')
The draws below stay inside these ranges and needn't reach their ends.
Inputs may be any that keep to these rules, and one draw needn't show every extreme that they name: `expert_ids`: the two experts of a token differ.
All inputs are finite; a program needn't handle non-finite values.
Results may differ from the reference program's by a relative error of at most 0.025.
Values may be sent and summed in bfloat16 or wider, within the bound.
No kernel may reach another device: no remote copies, remote signals or barrier semaphores. Data moves between devices by JAX's collectives and lax.ppermute only.
A program may use at most 64 MiB of HBM per device.

```python
import math
import jax
import jax.numpy as jnp
from jax import lax

D = 4096
EXPERTS = 8
RANK = 16
COND = 256
TASKS = 2
BLOCKS = 2
TOK_DEV = 16
MICRO = 4
TOKENS = 1024
N_SECTION = 4
N_DP = 64


def touch_ends(drawn, stream_key, least, top_value):
    longest = drawn.shape.index(max(drawn.shape))
    spots = []
    for shift in (0, 1):
        where = [jax.random.randint(jax.random.fold_in(stream_key, axis), (), 0, length) for axis, length in enumerate(drawn.shape)]
        where[longest] = (where[longest] + shift) % drawn.shape[longest]
        spots.append(tuple(where))
    return drawn.at[spots[0]].set(least).at[spots[1]].set(top_value)


def block_levels(own_key, shape, cuts, low, largest):
    loudness = 1.0
    for dim, shards_of in cuts:
        steps = jax.random.uniform(jax.random.fold_in(jax.random.fold_in(own_key, 6), dim), (shards_of,), jnp.float32, low / len(cuts), largest / len(cuts))
        loudness = loudness * jnp.repeat(jnp.exp(steps), shape[dim] // shards_of).reshape((-1,) + (1,) * (len(shape) - 1 - dim))
    return loudness


def different_ones(own_key, rows, count, top, lift):
    sequence = jax.random.permutation(jax.random.fold_in(own_key, 1), count)
    boost = sequence
    for power in range(3):
        boost = boost * boost // count
    boost = boost * lift // count
    lots = jax.random.randint(jax.random.fold_in(own_key, 2), (rows, count), 0, 4096) + boost
    holders = jax.random.permutation(jax.random.fold_in(own_key, 3), rows)[jnp.arange(count) % rows]
    lots = jnp.where(jnp.arange(rows)[:, None] == holders[None, :], 1 << 14, lots)
    score = lots * count + jnp.arange(count)
    return lax.top_k(score.astype(jnp.int32), top)[1].astype(jnp.int32)


def noise(rng, shape, width, reach, shards=(), held_as=jnp.bfloat16):
    values = width * jax.random.normal(rng, shape, jnp.float32)
    if shards:
        values = values * block_levels(rng, shape, shards, -0.22, 0.18)
    return jnp.clip(values, -reach, reach).astype(held_as)


def setup_inputs(seed: int = 0) -> dict:
    keys = jax.random.split(jax.random.key(seed), 10)
    return {
        "hidden_in": noise(keys[0], (BLOCKS, N_SECTION, MICRO, TOKENS, D), 1.0, 6.0, ((1, 4), (3, 64))),
        "out_grad": noise(keys[1], (MICRO, TOKENS, D), 1.0, 6.0, ((1, 64),)),
        "gate_probs": jnp.clip(jnp.exp(math.log(1.0) - 2.3025851 * jax.random.uniform(keys[2], (BLOCKS, N_SECTION, MICRO, TOKENS, 2), jnp.float32) ** block_levels(keys[2], (BLOCKS, N_SECTION, MICRO, TOKENS, 2), ((1, 4), (3, 64)), -0.2, 0.2)), 0.1, 1.0),
        "expert_ids": different_ones(keys[3], BLOCKS * N_SECTION * MICRO * TOKENS, EXPERTS, 2, 2048).reshape((BLOCKS, N_SECTION, MICRO, TOKENS, 2)),
        "task_ids": touch_ends(jax.random.randint(keys[4], (MICRO, N_DP), 0, TASKS), jax.random.fold_in(keys[4], 1), 0, TASKS - 1).astype(jnp.int32),
        "task_embed": noise(keys[5], (TASKS, COND), 1.0, 5.0, (), jnp.float32),
        "slot_embed": noise(keys[6], (BLOCKS, N_SECTION, EXPERTS, COND), 1.0, 5.0, ((1, 4),), jnp.float32),
        "gen_down": noise(keys[7], (COND, RANK * D), (COND * D // 2) ** -0.5, 0.0078125, ((1, 64),)),
        "gen_up": noise(keys[8], (COND, RANK * D), (COND * RANK) ** -0.5, 0.09375, ((1, 64),)),
    }


eps = 1e-05

def column_weights(gates, choices_ids, task_hot, experts, rank):
    expert_hot = (choices_ids[:, :, None] == jnp.arange(experts, dtype=jnp.int32)).astype(jnp.float32)
    per_expert = lax.optimization_barrier(jnp.sum(gates[:, :, None] * expert_hot, axis=1))
    table = task_hot[:, :, None] * per_expert[:, None, :]
    return jnp.repeat(table.reshape(table.shape[0], -1), rank, axis=1)

def layer_back(saved, cot_in, adapt_a, adapt_b, columns):
    values = saved.astype(jnp.float32)
    inv_rms = lax.rsqrt(lax.optimization_barrier(jnp.mean(values * values, axis=-1, keepdims=True)) + eps)
    normed_f = values * inv_rms
    normed = normed_f.astype(jnp.bfloat16)
    contract = (((1,), (1,)), ((), ()))
    low = lax.dot_general(normed, adapt_a, contract, preferred_element_type=jnp.float32)
    mixed_low = (columns * low).astype(jnp.bfloat16)
    back_low = lax.dot_general(cot_in, adapt_b, contract, preferred_element_type=jnp.float32)
    grad_low = (columns * back_low).astype(jnp.bfloat16)
    grad_norm = jnp.dot(grad_low, adapt_a, preferred_element_type=jnp.float32)
    grad_in = inv_rms * (grad_norm - normed_f * lax.optimization_barrier(jnp.mean(grad_norm * normed_f, axis=-1, keepdims=True)))
    result = (cot_in.astype(jnp.float32) + grad_in).astype(jnp.bfloat16)
    return (result, normed, mixed_low, grad_low)

def reference(hidden_in, out_grad, gate_probs, expert_ids, task_ids, task_embed, slot_embed, gen_down, gen_up):
    high = lax.Precision.HIGHEST
    combos = TASKS * EXPERTS
    pre_act = task_embed[None, None, :, None, :] + slot_embed[:, :, None, :, :]
    conditions = jax.nn.silu(pre_act).reshape(BLOCKS, N_SECTION, combos, COND)
    gen_a = jnp.einsum('jscw,wf->jscf', conditions, gen_down.astype(jnp.float32), precision=high).astype(jnp.bfloat16)
    gen_b = jnp.einsum('jscw,wf->jscf', conditions, gen_up.astype(jnp.float32), precision=high).astype(jnp.bfloat16)
    adapt_a = gen_a.reshape(BLOCKS, N_SECTION, combos * RANK, D)
    adapt_b = gen_b.reshape(BLOCKS, N_SECTION, combos * RANK, D)
    token_task = jnp.repeat(task_ids, TOK_DEV, axis=1).reshape(-1)
    task_hot = (token_task[:, None] == jnp.arange(TASKS, dtype=jnp.int32)).astype(jnp.float32)
    rows_contract = (((0,), (0,)), ((), ()))
    cot_now = out_grad.reshape(-1, D)
    grads_a = [[None] * N_SECTION for _ in range(BLOCKS)]
    grads_b = [[None] * N_SECTION for _ in range(BLOCKS)]
    hidden_out = [None] * N_SECTION
    for layer in reversed(range(BLOCKS * N_SECTION)):
        block_id, section_id = divmod(layer, N_SECTION)
        columns = column_weights(gate_probs[block_id, section_id].reshape(-1, 2), expert_ids[block_id, section_id].reshape(-1, 2), task_hot, EXPERTS, RANK)
        cot_prev = cot_now
        cot_now, normed, mixed_low, grad_low = layer_back(hidden_in[block_id, section_id].reshape(-1, D), cot_prev, adapt_a[block_id, section_id], adapt_b[block_id, section_id], columns)
        grads_a[block_id][section_id] = lax.dot_general(grad_low, normed, rows_contract, preferred_element_type=jnp.float32)
        grads_b[block_id][section_id] = lax.dot_general(mixed_low, cot_prev, rows_contract, preferred_element_type=jnp.float32)
        if block_id == 0:
            hidden_out[section_id] = cot_now.reshape(MICRO, TOKENS, D)
    grad_scale = 1.0 / (MICRO * TOKENS)
    full_a = jnp.stack([jnp.stack(line) for line in grads_a]).reshape(BLOCKS, N_SECTION, combos, RANK * D) * grad_scale
    full_b = jnp.stack([jnp.stack(line) for line in grads_b]).reshape(BLOCKS, N_SECTION, combos, RANK * D) * grad_scale
    d_gen_down = jnp.einsum('jscw,jscf->wf', conditions, full_a, precision=high)
    d_gen_up = jnp.einsum('jscw,jscf->wf', conditions, full_b, precision=high)
    d_cond = jnp.einsum('jscf,wf->jscw', full_a, gen_down.astype(jnp.float32), precision=high)
    d_cond = d_cond + jnp.einsum('jscf,wf->jscw', full_b, gen_up.astype(jnp.float32), precision=high)
    sigmoid_pre = jax.nn.sigmoid(pre_act)
    d_pre = d_cond.reshape(pre_act.shape) * sigmoid_pre * (1.0 + pre_act * (1.0 - sigmoid_pre))
    d_task = lax.optimization_barrier(jnp.sum(d_pre, axis=(0, 1, 3)))
    d_slot = lax.optimization_barrier(jnp.sum(d_pre, axis=2))
    return (jnp.stack(hidden_out), d_gen_down, d_gen_up, d_task, d_slot)
```

```python
import functools

import jax
import jax.numpy as jnp
from jax import lax
from jax.experimental import pallas as pl
from jax.experimental.pallas import tpu as pltpu
from jax.sharding import Mesh, PartitionSpec as P

eps = 1e-05
bf16 = jnp.bfloat16
f32 = jnp.float32

AXES = ("s", "x", "zh", "zl", "c")
DP = ("x", "zh", "zl", "c")
RANKS = ("x", "zh")
QUARTERS = ("zl", "c")
VMEM = pl.BlockSpec(memory_space=pltpu.VMEM)
SMEM = pl.BlockSpec(memory_space=pltpu.SMEM)
LAST = (((1,), (1,)), ((), ()))
FIRST = (((0,), (0,)), ((), ()))


def adapter_rows(g_ref, block, which, q):
    part = g_ref[:, q, block, which]
    return part.reshape(part.shape[0] * part.shape[1], part.shape[2])


def low_kernel(xn_ref, weights_ref, g_ref, out_ref):
    blocks = out_ref.shape[0]
    quarters, width = g_ref.shape[1], g_ref.shape[5]
    for j in range(blocks):
        low = jnp.zeros(out_ref.shape[1:], f32)
        for q in range(quarters):
            low += lax.dot_general(
                xn_ref[j, :, q * width : (q + 1) * width],
                adapter_rows(g_ref, j, 0, q),
                LAST,
                preferred_element_type=f32,
            )
        out_ref[j] = (weights_ref[j] * low).astype(bf16)


def tick_kernel(first, where_ref, *refs):
    if first:
        grad_ref, x_ref, inv_ref, weights_ref, g_ref, dx_ref, du_ref, cot_ref = refs
        cot_ref[...] = grad_ref[...]
    else:
        in_ref, x_ref, inv_ref, weights_ref, g_ref, dx_ref, du_ref = refs
        cot_ref = in_ref
    block, item = where_ref[0], where_ref[1]
    quarters, width = g_ref.shape[1], g_ref.shape[5]
    back = jnp.zeros(du_ref.shape, f32)
    for q in range(quarters):
        back += lax.dot_general(
            cot_ref[:, q * width : (q + 1) * width],
            adapter_rows(g_ref, block, 1, q),
            LAST,
            preferred_element_type=f32,
        )
    du = (weights_ref[item] * back).astype(bf16)
    du_ref[...] = du
    inv = inv_ref[item][:, :1]
    dxn, xf = [], []
    total = jnp.zeros((du.shape[0], 1), f32)
    for q in range(quarters):
        xf.append(x_ref[item, :, q * width : (q + 1) * width].astype(f32) * inv)
        dxn.append(
            jnp.dot(du, adapter_rows(g_ref, block, 0, q), preferred_element_type=f32)
        )
        total += jnp.sum(dxn[q] * xf[q], axis=1, keepdims=True)
    mean = total * (1.0 / (quarters * width))
    for q in range(quarters):
        cols = slice(q * width, (q + 1) * width)
        dx_ref[:, cols] = (
            cot_ref[:, cols].astype(f32) + inv * (dxn[q] - xf[q] * mean)
        ).astype(bf16)


def grads_kernel(mixed_ref, xn_ref, out_ref):
    width = xn_ref.shape[1]
    ranks, rows = out_ref.shape[0], out_ref.shape[1] // 2
    high = ranks * rows
    dy = mixed_ref[:, :width]
    du = mixed_ref[:, width : width + high]
    low = mixed_ref[:, width + high :]
    grad_a = lax.dot_general(du, xn_ref[...], FIRST, preferred_element_type=f32)
    out_ref[:, :rows, :] = grad_a.astype(bf16).reshape(ranks, rows, width)
    grad_b = lax.dot_general(low, dy, FIRST, preferred_element_type=f32)
    out_ref[:, rows:, :] = grad_b.astype(bf16).reshape(ranks, rows, width)


def call(kernel, out_shape, scalars, operands, flops, moved):
    return pl.pallas_call(
        kernel,
        out_shape=out_shape,
        in_specs=[SMEM] * scalars + [VMEM] * (len(operands) - scalars),
        out_specs=jax.tree.map(lambda _: VMEM, out_shape),
        compiler_params=pltpu.CompilerParams(vmem_limit_bytes=32 * 1024 * 1024),
        cost_estimate=pl.CostEstimate(flops=flops, bytes_accessed=moved, transcendentals=0),
    )(*operands)


def summed_over(part, axes):
    for axis in axes:
        part = jnp.sum(lax.all_gather(part, axis), axis=0)
    return part


def on_device(
    hidden_in, out_grad, gate_probs, expert_ids, task_ids, task_embed, slot_embed, gen_down, gen_up
):
    high = lax.Precision.HIGHEST
    sections = lax.axis_size("s")
    section_id = lax.axis_index("s")
    quarters = lax.axis_size(QUARTERS)
    ranks = lax.axis_size(RANKS)
    blocks, _, micros, rows, model = hidden_in.shape
    tasks, cond_width = task_embed.shape
    experts = slot_embed.shape[2]
    combos = tasks * experts
    width = model // quarters
    wide = ranks * combos
    items = blocks * micros
    tokens = micros * rows

    pre = task_embed[None, :, None, :] + slot_embed[:, 0][:, None, :, :]
    cond = jax.nn.silu(pre).reshape(blocks, combos, cond_width)
    gen_a = jnp.einsum("jcw,wf->jcf", cond, gen_down.astype(f32), precision=high).astype(bf16)
    gen_b = jnp.einsum("jcw,wf->jcf", cond, gen_up.astype(f32), precision=high).astype(bf16)
    mine = jnp.stack([gen_a, gen_b], axis=1).reshape(blocks * 2 * combos, width)
    filled = lax.all_gather(mine, DP, axis=0, tiled=True)
    adapters = filled.reshape(ranks, quarters, blocks, 2, combos, width)

    slots = lax.all_gather(slot_embed[:, 0], "s")
    pre_all = task_embed[None, None, :, None, :] + slots[:, :, None, :, :]
    cond_all = jax.nn.silu(pre_all).reshape(sections * blocks * combos, cond_width)
    saved = hidden_in[:, 0]
    values = saved.astype(f32)
    inv = lax.rsqrt(jnp.mean(values * values, axis=-1, keepdims=True) + eps)
    normed = (values * inv).astype(bf16).reshape(blocks, tokens, model)
    inv_items = jnp.broadcast_to(inv, (blocks, micros, rows, 128)).reshape(items, rows, 128)
    x_items = saved.reshape(items, rows, model)
    lane = jnp.arange(wide, dtype=jnp.int32)
    expert_of, task_of = lane % experts, (lane // experts) % tasks
    ids, gates = expert_ids[:, 0], gate_probs[:, 0]
    weights = jnp.where(ids[..., 0:1] == expert_of, gates[..., 0:1], 0.0) + jnp.where(
        ids[..., 1:2] == expert_of, gates[..., 1:2], 0.0
    )
    weights = jnp.where(task_ids[None, :, :, None] == task_of, weights, 0.0)
    weights_items = weights.reshape(items, rows, wide)
    normed_send = normed.reshape(blocks, tokens, quarters, width).transpose(2, 0, 1, 3)
    normed_quarter = lax.all_to_all(normed_send, QUARTERS, 0, 0)

    low = call(
        low_kernel,
        jax.ShapeDtypeStruct((blocks, tokens, wide), bf16),
        0,
        (normed, weights.reshape(blocks, tokens, wide), adapters),
        2 * blocks * tokens * wide * model,
        3 << 21,
    )

    def step(tick, incoming):
        position = jnp.clip(tick - (sections - 1 - section_id), 0, items - 1)
        block = blocks - 1 - position // micros
        item = block * micros + position % micros
        where = jnp.stack([block, item]).astype(jnp.int32)
        operands = (where, incoming, x_items, inv_items, weights_items, adapters)
        outs = call(
            functools.partial(tick_kernel, False),
            (
                jax.ShapeDtypeStruct((rows, model), bf16),
                jax.ShapeDtypeStruct((rows, wide), bf16),
            ),
            1,
            operands,
            4 * rows * wide * model,
            5 << 20,
        )
        return outs

    cots, dus, results = [], [], []
    incoming = jnp.zeros((rows, model), bf16)
    pairs = [(i, (i - 1) % sections) for i in range(sections)]
    reduced = [None] * blocks

    def layer_sum(block):
        start = (blocks - 1 - block) * micros
        def chosen(kept, m):
            return lax.select_n(
                section_id, *[kept[start + m + sections - 1 - s] for s in range(sections)]
            )
        dy = jnp.concatenate([chosen(cots, m) for m in range(micros)])
        du = jnp.concatenate([chosen(dus, m) for m in range(micros)])
        dy = dy.reshape(tokens, quarters, width).transpose(1, 0, 2)
        both = jnp.concatenate([du, low[block]], axis=1)
        both = jnp.broadcast_to(both[None], (quarters, tokens, 2 * wide))
        mixed = lax.all_to_all(jnp.concatenate([dy, both], axis=2), QUARTERS, 0, 0)
        part = call(
            grads_kernel,
            jax.ShapeDtypeStruct((ranks, 2 * combos, width), bf16),
            0,
            (
                mixed.reshape(quarters * tokens, width + 2 * wide),
                normed_quarter[:, block].reshape(quarters * tokens, width),
            ),
            4 * quarters * tokens * wide * width,
            3 << 20,
        )
        got = lax.all_to_all(part, RANKS, 0, 0)
        scale = 1.0 / (micros * rows * lax.axis_size(DP))
        return (jnp.sum(got.astype(f32), axis=0) * scale).astype(bf16)

    for tick in range(items + sections - 1):
        if tick < micros:
            fresh = section_id == sections - 1
            incoming = jnp.where(fresh, out_grad[tick], incoming)
        result, du = step(tick, incoming)
        cots.append(incoming)
        dus.append(du)
        results.append(result)
        if tick < items + sections - 2:
            incoming = lax.ppermute(result, "s", pairs)
        if tick == micros + sections - 2:
            reduced[1] = layer_sum(1)
    reduced[0] = layer_sum(0)

    hidden_out = jnp.stack(
        [
            lax.select_n(
                section_id,
                *[results[micros + m + sections - 1 - s] for s in range(sections)],
            )
            for m in range(micros)
        ]
    )
    all_layers = lax.all_gather(jnp.stack(reduced), "s")
    grads = all_layers.reshape(sections * blocks, 2, combos, width)
    grad_a = grads[:, 0].reshape(-1, width)
    grad_b = grads[:, 1].reshape(-1, width)
    d_cond = jnp.einsum("nf,wf->nw", grad_a, gen_down, preferred_element_type=f32)
    d_cond = d_cond + jnp.einsum("nf,wf->nw", grad_b, gen_up, preferred_element_type=f32)
    gate = jax.nn.sigmoid(pre_all)
    d_pre = d_cond.reshape(pre_all.shape) * gate * (1.0 + pre_all * (1.0 - gate))
    own = lax.dynamic_index_in_dim(d_pre, section_id, 0, keepdims=False)
    d_slot = jnp.sum(own, axis=1).reshape(blocks * experts, cond_width)
    d_task = jnp.sum(d_pre, axis=(0, 1, 3))
    small = summed_over(jnp.concatenate([d_slot, d_task]), (QUARTERS, "x", "zh"))
    d_slot = small[: blocks * experts].reshape(blocks, 1, experts, cond_width)
    d_task = small[blocks * experts :]
    d_gen_down = jnp.einsum("nw,nf->wf", cond_all, grad_a.astype(f32), precision=high)
    d_gen_up = jnp.einsum("nw,nf->wf", cond_all, grad_b.astype(f32), precision=high)
    return (hidden_out[None], d_gen_down, d_gen_up, d_task, d_slot)


def solution(mesh):
    split = Mesh(mesh.devices.reshape(mesh.devices.shape[0], 4, 4, 2, 2), AXES)
    placed = (
        P(None, "s", None, DP, None),
        P(None, DP, None),
        P(None, "s", None, DP, None),
        P(None, "s", None, DP, None),
        P(None, DP),
        P(),
        P(None, "s", None, None),
        P(None, DP),
        P(None, DP),
    )
    return jax.shard_map(
        on_device,
        mesh=split,
        in_specs=placed,
        out_specs=(
            P("s", None, DP, None),
            P(None, DP),
            P(None, DP),
            P(),
            P(None, "s", None, None),
        ),
        check_vma=False,
    )
```

```python
import functools

import jax
import jax.numpy as jnp
from jax import lax
from jax.experimental import pallas as pl
from jax.experimental.pallas import tpu as pltpu
from jax.sharding import Mesh, PartitionSpec as P

eps = 1e-05
bf16 = jnp.bfloat16
f32 = jnp.float32

AXES = ("s", "x", "zh", "zl", "c")
DP = ("x", "zh", "zl", "c")
RANKS = ("x", "zh")
QUARTERS = ("zl", "c")
VMEM = pl.BlockSpec(memory_space=pltpu.VMEM)
SMEM = pl.BlockSpec(memory_space=pltpu.SMEM)
LAST = (((1,), (1,)), ((), ()))
FIRST = (((0,), (0,)), ((), ()))
VMEM_LIMIT = 4 * 1024 * 1024


def adapter_rows(g_ref, block, which, q):
    part = g_ref[:, q, block, which]
    return part.reshape(part.shape[0] * part.shape[1], part.shape[2])


def prep_kernel(where_ref, x_ref, xn_ref, inv_ref, *sent):
    items, rows, model = x_ref.shape
    width = model // len(sent)
    for item in range(items):
        values = x_ref[item].astype(f32)
        inv = lax.rsqrt(jnp.mean(values * values, axis=1, keepdims=True) + eps)
        inv_ref[item] = jnp.broadcast_to(inv, (rows, inv_ref.shape[2]))
        xn_ref[item * rows : (item + 1) * rows, :] = (values * inv).astype(bf16)
    for d, out_ref in enumerate(sent):
        start = pl.multiple_of((where_ref[1] ^ d) * width, width)
        out_ref[...] = xn_ref[:, pl.ds(start, width)]


def low_kernel(xn_ref, weights_ref, g_ref, out_ref):
    blocks, tokens, _ = out_ref.shape
    quarters, width = g_ref.shape[1], g_ref.shape[5]
    for j in range(blocks):
        low = jnp.zeros(out_ref.shape[1:], f32)
        for q in range(quarters):
            low += lax.dot_general(
                xn_ref[j * tokens : (j + 1) * tokens, q * width : (q + 1) * width],
                adapter_rows(g_ref, j, 0, q),
                LAST,
                preferred_element_type=f32,
            )
        out_ref[j] = (weights_ref[j] * low).astype(bf16)


def tick_kernel(tick, sections, micros, where_ref, *refs):
    refs = list(refs)
    section = where_ref[0]
    if tick < micros:
        grad = refs.pop(0)[tick]
        if tick:
            cot = jnp.where(section == sections - 1, grad, refs.pop(0)[...])
        else:
            cot = grad
    else:
        cot = refs.pop(0)[...]
    x_ref, inv_ref, weights_ref, g_ref, dx_ref = refs[:5]
    sent = refs[5:]
    blocks, items = g_ref.shape[2], x_ref.shape[0]
    quarters, width = g_ref.shape[1], g_ref.shape[5]
    position = jnp.clip(tick - (sections - 1 - section), 0, items - 1)
    late = (position >= micros).astype(jnp.int32)
    block = blocks - 1 - late
    item = block * micros + position - late * micros
    back = jnp.zeros(weights_ref.shape[1:], f32)
    for q in range(quarters):
        back += lax.dot_general(
            cot[:, q * width : (q + 1) * width],
            adapter_rows(g_ref, block, 1, q),
            LAST,
            preferred_element_type=f32,
        )
    du = (weights_ref[item] * back).astype(bf16)
    inv = inv_ref[item][:, :1]
    dxn, xf = [], []
    total = jnp.zeros((du.shape[0], 1), f32)
    for q in range(quarters):
        xf.append(x_ref[item, :, q * width : (q + 1) * width].astype(f32) * inv)
        dxn.append(
            jnp.dot(du, adapter_rows(g_ref, block, 0, q), preferred_element_type=f32)
        )
        total += jnp.sum(dxn[q] * xf[q], axis=1, keepdims=True)
    mean = total * (1.0 / (quarters * width))
    for q in range(quarters):
        cols = slice(q * width, (q + 1) * width)
        dx_ref[:, cols] = (
            cot[:, cols].astype(f32) + inv * (dxn[q] - xf[q] * mean)
        ).astype(bf16)
    mine = where_ref[1]
    for d, out_ref in enumerate(sent):
        out_ref[:, width:] = du
        part = jnp.zeros((du.shape[0], width), bf16)
        for q in range(quarters):
            part = jnp.where((mine ^ d) == q, cot[:, q * width : (q + 1) * width], part)
        out_ref[:, :width] = part


def grads_kernel(block, micros, sections, quarters, where_ref, *refs):
    out_ref, mixed_ref = refs[-2:]
    ticks = micros + sections - 1
    kept = refs[: ticks * quarters]
    lows = refs[ticks * quarters : (ticks + 1) * quarters]
    xns = refs[(ticks + 1) * quarters : (ticks + 2) * quarters]
    rows, width = kept[0].shape[0], xns[0].shape[1]
    tokens = micros * rows
    ranks, combos = out_ref.shape[0], out_ref.shape[1] // 2
    section = where_ref[0]
    for d in range(quarters):
        for m in range(micros):
            value = kept[(m + sections - 1) * quarters + d][...]
            for s in range(1, sections):
                value = jnp.where(
                    section == s, kept[(m + sections - 1 - s) * quarters + d][...], value
                )
            at = d * tokens + m * rows
            mixed_ref[at : at + rows, :] = value
    xn = jnp.concatenate([ref[block * tokens : (block + 1) * tokens, :] for ref in xns])
    low = jnp.concatenate([ref[block] for ref in lows])
    grad_a = lax.dot_general(mixed_ref[:, width:], xn, FIRST, preferred_element_type=f32)
    out_ref[:, :combos, :] = grad_a.astype(bf16).reshape(ranks, combos, width)
    grad_b = lax.dot_general(low, mixed_ref[:, :width], FIRST, preferred_element_type=f32)
    out_ref[:, combos:, :] = grad_b.astype(bf16).reshape(ranks, combos, width)


def call(kernel, out_shape, operands, flops, moved, scratch=()):
    scalars = 1 if operands[0].dtype == jnp.int32 else 0
    return pl.pallas_call(
        kernel,
        out_shape=out_shape,
        in_specs=[SMEM] * scalars + [VMEM] * (len(operands) - scalars),
        out_specs=jax.tree.map(lambda _: VMEM, out_shape),
        scratch_shapes=scratch,
        compiler_params=pltpu.CompilerParams(vmem_limit_bytes=VMEM_LIMIT),
        cost_estimate=pl.CostEstimate(flops=flops, bytes_accessed=moved, transcendentals=0),
    )(*operands)


def swapped(parts, axes, unit=1):
    count = lax.axis_size(axes)
    return [parts[0]] + [
        lax.ppermute(part, axes, [(i, i ^ (d * unit)) for i in range(count)])
        for d, part in enumerate(parts)
        if d
    ]


def tree_sum(parts):
    while len(parts) > 1:
        parts = [parts[i] + parts[i + 1] for i in range(0, len(parts), 2)]
    return parts[0]


def from_sections(part):
    count = lax.axis_size("s")
    got = [part] + [
        lax.ppermute(part, "s", [((i + d) % count, i) for i in range(count)])
        for d in range(1, count)
    ]
    me = lax.axis_index("s")
    return jnp.stack([lax.select_n(lax.rem(i + count - me, count), *got) for i in range(count)])


def on_device(
    hidden_in, out_grad, gate_probs, expert_ids, task_ids, task_embed, slot_embed, gen_down, gen_up
):
    high = lax.Precision.HIGHEST
    sections = lax.axis_size("s")
    section_id = lax.axis_index("s")
    quarters = lax.axis_size(QUARTERS)
    ranks = lax.axis_size(RANKS)
    blocks, _, micros, rows, model = hidden_in.shape
    tasks, cond_width = task_embed.shape
    experts = slot_embed.shape[2]
    combos = tasks * experts
    width = model // quarters
    wide = ranks * combos
    items = blocks * micros
    tokens = micros * rows
    where = jnp.stack([section_id, lax.axis_index(QUARTERS)]).astype(jnp.int32)

    def shaped(*shape, dtype=bf16):
        return jax.ShapeDtypeStruct(shape, dtype)

    pre = task_embed[None, :, None, :] + slot_embed[:, 0][:, None, :, :]
    cond = jax.nn.silu(pre).reshape(blocks, combos, cond_width)
    gen_a = jnp.einsum("jcw,wf->jcf", cond, gen_down.astype(f32), precision=high).astype(bf16)
    gen_b = jnp.einsum("jcw,wf->jcf", cond, gen_up.astype(f32), precision=high).astype(bf16)
    mine = jnp.stack([gen_a, gen_b], axis=1).reshape(blocks * 2 * combos, width)
    filled = lax.all_gather(mine, DP, axis=0, tiled=True)

    slots = from_sections(slot_embed[:, 0])
    x_items = hidden_in[:, 0].reshape(items, rows, model)
    normed, inv_items, *sent = call(
        prep_kernel,
        [shaped(items * rows, model), shaped(items, rows, 128, dtype=f32)]
        + [shaped(items * rows, width)] * quarters,
        (where, x_items),
        8 * items * rows * model,
        3 << 20,
    )
    normed_quarter = swapped(sent, QUARTERS)
    lane = jnp.arange(wide, dtype=jnp.int32)
    expert_of, task_of = lane % experts, (lane // experts) % tasks
    ids, gates = expert_ids[:, 0], gate_probs[:, 0]
    weights = jnp.where(ids[..., 0:1] == expert_of, gates[..., 0:1], 0.0) + jnp.where(
        ids[..., 1:2] == expert_of, gates[..., 1:2], 0.0
    )
    weights = jnp.where(task_ids[None, :, :, None] == task_of, weights, 0.0)
    weights_items = weights.reshape(items, rows, wide)

    filled, slots, normed, inv_items, normed_quarter, weights_items = lax.optimization_barrier(
        (filled, slots, normed, inv_items, normed_quarter, weights_items)
    )
    adapters = filled.reshape(ranks, quarters, blocks, 2, combos, width)
    low = call(
        low_kernel,
        shaped(blocks, tokens, wide),
        (normed, weights_items.reshape(blocks, tokens, wide), adapters),
        2 * blocks * tokens * wide * model,
        3 << 21,
    )
    lows = swapped([low] * quarters, QUARTERS)

    kept, results = [], []
    incoming = None
    pairs = [(i, (i - 1) % sections) for i in range(sections)]
    reduced = [None] * blocks

    def exchanged(block):
        start = (blocks - 1 - block) * micros
        used = [part for parts in kept[start : start + micros + sections - 1] for part in parts]
        part = call(
            functools.partial(grads_kernel, block, micros, sections, quarters),
            shaped(ranks, 2 * combos, width),
            (where, *used, *lows, *normed_quarter),
            4 * quarters * tokens * wide * width,
            5 << 20,
            [pltpu.VMEM((quarters * tokens, width + wide), bf16)],
        )
        return lax.all_to_all(part, RANKS, 0, 0)

    def summed(got):
        scale = 1.0 / (micros * rows * lax.axis_size(DP))
        return (jnp.sum(got.astype(f32), axis=0) * scale).astype(bf16)

    for tick in range(items + sections - 1):
        operands = [where]
        if tick < micros:
            operands.append(out_grad)
        if tick:
            operands.append(incoming)
        result, *sent = call(
            functools.partial(tick_kernel, tick, sections, micros),
            [shaped(rows, model)] + [shaped(rows, width + wide)] * quarters,
            (*operands, x_items, inv_items, weights_items, adapters),
            4 * rows * wide * model,
            5 << 20,
        )
        results.append(result)
        if tick < items + sections - 2:
            incoming = lax.ppermute(result, "s", pairs)
        kept.append(swapped(sent, QUARTERS))
        if tick == micros + sections - 2:
            early = exchanged(1)
    late = exchanged(0)
    reduced = jnp.stack([summed(late), summed(early)])

    hidden_out = jnp.stack(
        [
            lax.select_n(
                section_id,
                *[results[micros + m + sections - 1 - s] for s in range(sections)],
            )
            for m in range(micros)
        ]
    )
    pre_all = task_embed[None, None, :, None, :] + slots[:, :, None, :, :]
    cond_all = jax.nn.silu(pre_all).reshape(sections * blocks * combos, cond_width)
    grads = from_sections(reduced).reshape(sections * blocks, 2, combos, width)
    grad_a = grads[:, 0].reshape(-1, width)
    grad_b = grads[:, 1].reshape(-1, width)
    d_cond = jnp.einsum("nf,wf->nw", grad_a, gen_down, preferred_element_type=f32)
    d_cond = d_cond + jnp.einsum("nf,wf->nw", grad_b, gen_up, preferred_element_type=f32)
    gate = jax.nn.sigmoid(pre_all)
    d_pre = d_cond.reshape(pre_all.shape) * gate * (1.0 + pre_all * (1.0 - gate))
    own = lax.dynamic_index_in_dim(d_pre, section_id, 0, keepdims=False)
    d_slot = jnp.sum(own, axis=1).reshape(blocks * experts, cond_width)
    d_task = jnp.sum(d_pre, axis=(0, 1, 3))
    small = jnp.concatenate([d_slot, d_task])
    small = tree_sum(swapped([small] * 8, DP))
    small = tree_sum(swapped([small] * 8, DP, 8))
    d_slot = small[: blocks * experts].reshape(blocks, 1, experts, cond_width)
    d_task = small[blocks * experts :]
    d_gen_down = jnp.einsum("nw,nf->wf", cond_all, grad_a.astype(f32), precision=high)
    d_gen_up = jnp.einsum("nw,nf->wf", cond_all, grad_b.astype(f32), precision=high)
    return (hidden_out[None], d_gen_down, d_gen_up, d_task, d_slot)


def solution(mesh):
    split = Mesh(mesh.devices.reshape(mesh.devices.shape[0], 4, 4, 2, 2), AXES)
    placed = (
        P(None, "s", None, DP, None),
        P(None, DP, None),
        P(None, "s", None, DP, None),
        P(None, "s", None, DP, None),
        P(None, DP),
        P(),
        P(None, "s", None, None),
        P(None, DP),
        P(None, DP),
    )
    return jax.shard_map(
        on_device,
        mesh=split,
        in_specs=placed,
        out_specs=(
            P("s", None, DP, None),
            P(None, DP),
            P(None, DP),
            P(),
            P(None, "s", None, None),
        ),
        check_vma=False,
    )
```

```python
import functools

import jax
import jax.numpy as jnp
from jax import lax
from jax.experimental import pallas as pl
from jax.experimental.pallas import tpu as pltpu
from jax.sharding import Mesh, PartitionSpec as P

eps = 1e-05
bf16 = jnp.bfloat16
f32 = jnp.float32

AXES = ("s", "x", "zh", "zl", "c")
DP = ("x", "zh", "zl", "c")
RANKS = ("x", "zh")
QUARTERS = ("zl", "c")
VMEM = pl.BlockSpec(memory_space=pltpu.VMEM)
SMEM = pl.BlockSpec(memory_space=pltpu.SMEM)
LAST = (((1,), (1,)), ((), ()))
FIRST = (((0,), (0,)), ((), ()))
VMEM_LIMIT = 6 * 1024 * 1024
ADAPTER_LIMIT = 53 * 1024 * 1024


def adapter_copies(g_ref, block, which, held_ref, sems):
    return [
        pltpu.make_async_copy(g_ref.at[:, q, block, which], held_ref.at[q], sems.at[q])
        for q in range(g_ref.shape[1])
    ]


def adapter_rows(held_ref, q):
    part = held_ref[q]
    return part.reshape(part.shape[0] * part.shape[1], part.shape[2])


def prep_kernel(x_ref, xn_ref, inv_ref, sent_ref):
    items, rows, _ = x_ref.shape
    width = sent_ref.shape[2]
    for item in range(items):
        values = x_ref[item].astype(f32)
        inv = lax.rsqrt(jnp.mean(values * values, axis=1, keepdims=True) + eps)
        inv_ref[item] = jnp.broadcast_to(inv, (rows, inv_ref.shape[2]))
        normed = (values * inv).astype(bf16)
        where = slice(item * rows, (item + 1) * rows)
        xn_ref[where, :] = normed
        for q in range(sent_ref.shape[0]):
            sent_ref[q, where, :] = normed[:, q * width : (q + 1) * width]


def low_kernel(xn_ref, weights_ref, g_ref, out_ref, held_ref, sems):
    blocks, tokens, _ = out_ref.shape
    quarters, width = g_ref.shape[1], g_ref.shape[5]
    copies = [adapter_copies(g_ref, j, 0, held_ref.at[j], sems.at[j]) for j in range(blocks)]
    for copy in sum(copies, []):
        copy.start()
    for j in range(blocks):
        low = jnp.zeros(out_ref.shape[1:], f32)
        for q in range(quarters):
            copies[j][q].wait()
            low += lax.dot_general(
                xn_ref[j * tokens : (j + 1) * tokens, q * width : (q + 1) * width],
                adapter_rows(held_ref.at[j], q),
                LAST,
                preferred_element_type=f32,
            )
        out_ref[j] = (weights_ref[j] * low).astype(bf16)


def tick_kernel(tick, sections, micros, where_ref, *refs):
    refs = list(refs)
    x_ref, inv_ref, weights_ref, g_ref, dx_ref, du_ref, held_ref, sems = refs[-8:]
    blocks, items = g_ref.shape[2], x_ref.shape[0]
    quarters, width = g_ref.shape[1], g_ref.shape[5]
    section = where_ref[0]
    position = jnp.clip(tick - (sections - 1 - section), 0, items - 1)
    late = (position >= micros).astype(jnp.int32)
    block = blocks - 1 - late
    item = block * micros + position - late * micros
    copies = [adapter_copies(g_ref, block, i, held_ref.at[i], sems.at[i]) for i in (0, 1)]
    for copy in copies[1] + copies[0]:
        copy.start()
    if tick < micros:
        grad = refs.pop(0)[tick]
        if tick:
            cot = jnp.where(section == sections - 1, grad, refs.pop(0)[...])
        else:
            cot = grad
    else:
        cot = refs.pop(0)[...]
    back = jnp.zeros(du_ref.shape, f32)
    for q in range(quarters):
        copies[1][q].wait()
        back += lax.dot_general(
            cot[:, q * width : (q + 1) * width],
            adapter_rows(held_ref.at[1], q),
            LAST,
            preferred_element_type=f32,
        )
    du = (weights_ref[item] * back).astype(bf16)
    du_ref[...] = du
    inv = inv_ref[item][:, :1]
    dxn, xf = [], []
    total = jnp.zeros((du.shape[0], 1), f32)
    for q in range(quarters):
        xf.append(x_ref[item, :, q * width : (q + 1) * width].astype(f32) * inv)
        copies[0][q].wait()
        dxn.append(jnp.dot(du, adapter_rows(held_ref.at[0], q), preferred_element_type=f32))
        total += jnp.sum(dxn[q] * xf[q], axis=1, keepdims=True)
    mean = total * (1.0 / (quarters * width))
    for q in range(quarters):
        cols = slice(q * width, (q + 1) * width)
        dx_ref[:, cols] = (
            cot[:, cols].astype(f32) + inv * (dxn[q] - xf[q] * mean)
        ).astype(bf16)


def pack_kernel(block, micros, sections, fresh, where_ref, low_ref, *refs):
    out_ref = refs[-1]
    grad_ref = refs[0]
    cots, dus = refs[1 : sections + micros], refs[sections + micros : -1]
    quarters, tokens, _ = out_ref.shape
    rows, wide = dus[0].shape
    width = cots[0].shape[1] // quarters
    section = where_ref[0]
    for m in range(micros):
        cot = grad_ref[m] if fresh else cots[m][...]
        du = dus[m][...]
        for s in range(sections - 1):
            at = m + sections - 1 - s
            cot = jnp.where(section == s, cots[at][...], cot)
            du = jnp.where(section == s, dus[at][...], du)
        where = slice(m * rows, (m + 1) * rows)
        for q in range(quarters):
            out_ref[q, where, :width] = cot[:, q * width : (q + 1) * width]
            out_ref[q, where, width : width + wide] = du
    for q in range(quarters):
        out_ref[q, :, width + wide :] = low_ref[block]


def grads_kernel(block, mixed_ref, xn_ref, out_ref):
    quarters, _, width = xn_ref.shape
    tokens = mixed_ref.shape[0] // quarters
    ranks, combos = out_ref.shape[0], out_ref.shape[1] // 2
    wide = ranks * combos
    xn = jnp.concatenate(
        [xn_ref[q, block * tokens : (block + 1) * tokens, :] for q in range(quarters)]
    )
    dy = mixed_ref[:, :width]
    du = mixed_ref[:, width : width + wide]
    low = mixed_ref[:, width + wide :]
    grad_a = lax.dot_general(du, xn, FIRST, preferred_element_type=f32)
    out_ref[:, :combos, :] = grad_a.astype(bf16).reshape(ranks, combos, width)
    grad_b = lax.dot_general(low, dy, FIRST, preferred_element_type=f32)
    out_ref[:, combos:, :] = grad_b.astype(bf16).reshape(ranks, combos, width)


def generate_kernel(cond_ref, down_ref, up_ref, out_ref):
    blocks, _, combos, _ = out_ref.shape
    cond = cond_ref[...]
    first = cond.astype(bf16)
    rest = cond - first.astype(f32)
    second = rest.astype(bf16)
    third = (rest - second.astype(f32)).astype(bf16)
    parts = jnp.concatenate([first, second, third])
    rows = cond.shape[0]
    for which, gen_ref in enumerate((down_ref, up_ref)):
        made = jnp.dot(parts, gen_ref[...], preferred_element_type=f32)
        made = made[:rows] + (made[rows : 2 * rows] + made[2 * rows :])
        out_ref[:, which] = made.astype(bf16).reshape(blocks, combos, -1)


def call(kernel, out_shape, operands, flops, moved, adapters=None):
    scalars = 1 if operands[0].dtype == jnp.int32 else 0
    specs = [SMEM] * scalars + [VMEM] * (len(operands) - scalars)
    scratch = []
    if adapters is not None:
        ranks, quarters, _, _, combos, width = adapters.shape
        operands = (*operands, adapters)
        specs.append(pl.BlockSpec(memory_space=pltpu.HBM))
        scratch = [
            pltpu.VMEM((2, quarters, ranks, combos, width), bf16),
            pltpu.SemaphoreType.DMA((2, quarters)),
        ]
    return pl.pallas_call(
        kernel,
        out_shape=out_shape,
        in_specs=specs,
        out_specs=jax.tree.map(lambda _: VMEM, out_shape),
        scratch_shapes=scratch,
        compiler_params=pltpu.CompilerParams(
            vmem_limit_bytes=VMEM_LIMIT if adapters is None else ADAPTER_LIMIT
        ),
        cost_estimate=pl.CostEstimate(flops=flops, bytes_accessed=moved, transcendentals=0),
    )(*operands)


def from_sections(part):
    count = lax.axis_size("s")
    got = [part] + [
        lax.ppermute(part, "s", [((i + d) % count, i) for i in range(count)])
        for d in range(1, count)
    ]
    me = lax.axis_index("s")
    return jnp.stack([lax.select_n(lax.rem(i + count - me, count), *got) for i in range(count)])


def on_device(
    hidden_in, out_grad, gate_probs, expert_ids, task_ids, task_embed, slot_embed, gen_down, gen_up
):
    high = lax.Precision.HIGHEST
    sections = lax.axis_size("s")
    section_id = lax.axis_index("s")
    quarters = lax.axis_size(QUARTERS)
    ranks = lax.axis_size(RANKS)
    blocks, _, micros, rows, model = hidden_in.shape
    tasks, cond_width = task_embed.shape
    experts = slot_embed.shape[2]
    combos = tasks * experts
    width = model // quarters
    wide = ranks * combos
    items = blocks * micros
    tokens = micros * rows
    where = section_id.reshape(1).astype(jnp.int32)

    def shaped(*shape, dtype=bf16):
        return jax.ShapeDtypeStruct(shape, dtype)

    pre = task_embed[None, :, None, :] + slot_embed[:, 0][:, None, :, :]
    cond = jax.nn.silu(pre).reshape(blocks, combos, cond_width)
    mine = call(
        generate_kernel,
        shaped(blocks, 2, combos, width),
        (cond.reshape(blocks * combos, cond_width), gen_down, gen_up),
        12 * blocks * combos * cond_width * width,
        5 << 18,
    )
    filled = lax.all_gather(mine.reshape(blocks * 2 * combos, width), DP, axis=0, tiled=True)

    slots = from_sections(slot_embed[:, 0])
    x_items = hidden_in[:, 0].reshape(items, rows, model)
    normed, inv_items, sent = call(
        prep_kernel,
        [
            shaped(items * rows, model),
            shaped(items, rows, 128, dtype=f32),
            shaped(quarters, items * rows, width),
        ],
        (x_items,),
        8 * items * rows * model,
        3 << 20,
    )
    normed_quarter = lax.all_to_all(sent, QUARTERS, 0, 0)
    lane = jnp.arange(wide, dtype=jnp.int32)
    expert_of, task_of = lane % experts, (lane // experts) % tasks
    ids, gates = expert_ids[:, 0], gate_probs[:, 0]
    weights = jnp.where(ids[..., 0:1] == expert_of, gates[..., 0:1], 0.0) + jnp.where(
        ids[..., 1:2] == expert_of, gates[..., 1:2], 0.0
    )
    weights = jnp.where(task_ids[None, :, :, None] == task_of, weights, 0.0)
    weights_items = weights.reshape(items, rows, wide)

    filled, slots, normed, inv_items, normed_quarter, weights_items = lax.optimization_barrier(
        (filled, slots, normed, inv_items, normed_quarter, weights_items)
    )
    adapters = filled.reshape(ranks, quarters, blocks, 2, combos, width)
    pairs = [(i, (i - 1) % sections) for i in range(sections)]
    last = items + sections - 2

    def packed(block):
        span = slice((blocks - 1 - block) * micros, (blocks - block) * micros + sections - 1)
        fresh = block == blocks - 1
        cots = [out_grad[0] if cot is None else cot for cot in incoming[span]]
        return call(
            functools.partial(pack_kernel, block, micros, sections, fresh),
            shaped(quarters, tokens, width + 2 * wide),
            (where, low, out_grad, *cots, *dus[span]),
            0,
            3 << 20,
        )

    def partial_grads(block, mixed):
        return call(
            functools.partial(grads_kernel, block),
            shaped(ranks, 2 * combos, width),
            (mixed.reshape(quarters * tokens, width + 2 * wide), normed_quarter),
            4 * quarters * tokens * wide * width,
            5 << 20,
        )

    def summed(got):
        scale = 1.0 / (micros * rows * lax.axis_size(DP))
        return (jnp.sum(got.astype(f32), axis=0) * scale).astype(bf16)

    incoming, dus, results = [None], [], []
    for tick in range(last + 1):
        operands = [where]
        if tick < micros:
            operands.append(out_grad)
        if tick:
            operands.append(incoming[tick])
        result, du = call(
            functools.partial(tick_kernel, tick, sections, micros),
            [shaped(rows, model), shaped(rows, wide)],
            (*operands, x_items, inv_items, weights_items),
            4 * rows * wide * model,
            5 << 20,
            adapters,
        )
        results.append(result)
        dus.append(du)
        if tick == last:
            break
        arriving = lax.ppermute(result, "s", pairs)
        if tick == 1:
            low = call(
                low_kernel,
                shaped(blocks, tokens, wide),
                (normed, weights_items.reshape(blocks, tokens, wide)),
                2 * blocks * tokens * wide * model,
                3 << 21,
                adapters,
            )
            arriving, low = lax.optimization_barrier((arriving, low))
        if tick == micros + sections - 2:
            mixed = lax.all_to_all(packed(1), QUARTERS, 0, 0)
        if tick == micros + sections - 1:
            early = partial_grads(1, mixed)
            arriving, early = lax.optimization_barrier((arriving, early))
            early_got = lax.all_to_all(early, RANKS, 0, 0)
        incoming.append(arriving)
    late, early_got = lax.optimization_barrier((packed(0), early_got))
    mixed = lax.all_to_all(late, QUARTERS, 0, 0)
    late_got = lax.all_to_all(partial_grads(0, mixed), RANKS, 0, 0)

    hidden_out = jnp.stack(
        [
            lax.select_n(
                section_id,
                *[results[micros + m + sections - 1 - s] for s in range(sections)],
            )
            for m in range(micros)
        ]
    )
    hidden_out, late_got = lax.optimization_barrier((hidden_out, late_got))
    reduced = jnp.stack([summed(late_got), summed(early_got)])
    pre_all = task_embed[None, None, :, None, :] + slots[:, :, None, :, :]
    cond_all = jax.nn.silu(pre_all).reshape(sections * blocks * combos, cond_width)
    grads = from_sections(reduced).reshape(sections * blocks, 2, combos, width)
    grad_a = grads[:, 0].reshape(-1, width)
    grad_b = grads[:, 1].reshape(-1, width)
    d_cond = jnp.einsum("nf,wf->nw", grad_a, gen_down, preferred_element_type=f32)
    d_cond = d_cond + jnp.einsum("nf,wf->nw", grad_b, gen_up, preferred_element_type=f32)
    gate = jax.nn.sigmoid(pre_all)
    d_pre = d_cond.reshape(pre_all.shape) * gate * (1.0 + pre_all * (1.0 - gate))
    own = lax.dynamic_index_in_dim(d_pre, section_id, 0, keepdims=False)
    d_slot = jnp.sum(own, axis=1).reshape(blocks * experts, cond_width)
    d_task = jnp.sum(d_pre, axis=(0, 1, 3))
    small = jnp.concatenate([d_slot, d_task])
    held = small.reshape(-1, 128)
    held = jnp.pad(held, ((0, -held.shape[0] % 8), (0, 0)))
    for axes in (QUARTERS, "x", "zh"):
        got = lax.all_gather(held, axes, axis=0, tiled=True)
        held = jnp.sum(got.reshape(-1, *held.shape), axis=0)
    small = held[: small.size // 128].reshape(small.shape)
    d_slot = small[: blocks * experts].reshape(blocks, 1, experts, cond_width)
    d_task = small[blocks * experts :]
    d_gen_down = jnp.einsum("nw,nf->wf", cond_all, grad_a.astype(f32), precision=high)
    d_gen_up = jnp.einsum("nw,nf->wf", cond_all, grad_b.astype(f32), precision=high)
    return (hidden_out[None], d_gen_down, d_gen_up, d_task, d_slot)


def solution(mesh):
    split = Mesh(mesh.devices.reshape(mesh.devices.shape[0], 4, 4, 2, 2), AXES)
    placed = (
        P(None, "s", None, DP, None),
        P(None, DP, None),
        P(None, "s", None, DP, None),
        P(None, "s", None, DP, None),
        P(None, DP),
        P(),
        P(None, "s", None, None),
        P(None, DP),
        P(None, DP),
    )
    return jax.shard_map(
        on_device,
        mesh=split,
        in_specs=placed,
        out_specs=(
            P("s", None, DP, None),
            P(None, DP),
            P(None, DP),
            P(),
            P(None, "s", None, None),
        ),
        check_vma=False,
    )
```

```python
import functools

import jax
import jax.numpy as jnp
from jax import lax
from jax.experimental import pallas as pl
from jax.experimental.pallas import tpu as pltpu
from jax.sharding import Mesh, PartitionSpec as P

eps = 1e-05
bf16 = jnp.bfloat16
f32 = jnp.float32

AXES = ("s", "x", "zh", "zl", "c")
DP = ("x", "zh", "zl", "c")
RANKS = ("x", "zh")
QUARTERS = ("zl", "c")
VMEM = pl.BlockSpec(memory_space=pltpu.VMEM)
SMEM = pl.BlockSpec(memory_space=pltpu.SMEM)
LAST = (((1,), (1,)), ((), ()))
FIRST = (((0,), (0,)), ((), ()))
VMEM_LIMIT = 4 * 1024 * 1024


def adapter_rows(g_ref, which, q):
    part = g_ref[:, q, which]
    return part.reshape(part.shape[0] * part.shape[1], part.shape[2])


def chosen_quarter(value, index, quarters):
    width = value.shape[1] // quarters
    part = value[:, :width]
    for q in range(1, quarters):
        part = jnp.where(index == q, value[:, q * width : (q + 1) * width], part)
    return part


def prep_kernel(where_ref, x_ref, xn_ref, inv_ref, *sent):
    items, rows, _ = x_ref.shape
    for item in range(items):
        values = x_ref[item].astype(f32)
        inv = lax.rsqrt(jnp.mean(values * values, axis=1, keepdims=True) + eps)
        inv_ref[item] = jnp.broadcast_to(inv, (rows, inv_ref.shape[2]))
        normed = (values * inv).astype(bf16)
        where = slice(item * rows, (item + 1) * rows)
        xn_ref[where, :] = normed
        for d, out_ref in enumerate(sent):
            out_ref[where, :] = chosen_quarter(normed, where_ref[1] ^ d, len(sent))


def low_kernel(block, xn_ref, weights_ref, g_ref, out_ref):
    tokens, _ = out_ref.shape
    quarters, width = g_ref.shape[1], g_ref.shape[4]
    low = jnp.zeros(out_ref.shape, f32)
    for q in range(quarters):
        low += lax.dot_general(
            xn_ref[block * tokens : (block + 1) * tokens, q * width : (q + 1) * width],
            adapter_rows(g_ref, 0, q),
            LAST,
            preferred_element_type=f32,
        )
    weights = weights_ref[block * tokens : (block + 1) * tokens, :]
    out_ref[...] = (weights * low).astype(bf16)


def tick_kernel(tick, sections, micros, where_ref, *refs):
    refs = list(refs)
    section = where_ref[0]
    if tick < micros:
        grad = refs.pop(0)[tick]
        if tick:
            cot = jnp.where(section == sections - 1, grad, refs.pop(0)[...])
        else:
            cot = grad
    else:
        cot = refs.pop(0)[...]
    x_ref, inv_ref, weights_ref = refs[:3]
    dx_ref, du_ref = refs[-2:]
    adapters = refs[3:-2]
    position = jnp.clip(tick - (sections - 1 - section), 0, x_ref.shape[0] - 1)

    def layer(block, g_ref, item):
        quarters, width = g_ref.shape[1], g_ref.shape[4]
        back = jnp.zeros(du_ref.shape, f32)
        for q in range(quarters):
            back += lax.dot_general(
                cot[:, q * width : (q + 1) * width],
                adapter_rows(g_ref, 1, q),
                LAST,
                preferred_element_type=f32,
            )
        du = (weights_ref[item] * back).astype(bf16)
        du_ref[...] = du
        inv = inv_ref[item][:, :1]
        dxn, xf = [], []
        total = jnp.zeros((du.shape[0], 1), f32)
        for q in range(quarters):
            xf.append(x_ref[item, :, q * width : (q + 1) * width].astype(f32) * inv)
            dxn.append(jnp.dot(du, adapter_rows(g_ref, 0, q), preferred_element_type=f32))
            total += jnp.sum(dxn[q] * xf[q], axis=1, keepdims=True)
        mean = total * (1.0 / (quarters * width))
        for q in range(quarters):
            cols = slice(q * width, (q + 1) * width)
            dx_ref[:, cols] = (
                cot[:, cols].astype(f32) + inv * (dxn[q] - xf[q] * mean)
            ).astype(bf16)

    if tick < micros:
        layer(1, adapters[0], micros + position)
    elif tick >= micros + sections - 1:
        layer(0, adapters[0], position - micros)
    else:
        pl.when(position < micros)(lambda: layer(1, adapters[0], micros + position))
        pl.when(position >= micros)(lambda: layer(0, adapters[1], position - micros))


def pack_kernel(micros, sections, fresh, where_ref, low_ref, *refs):
    spans = micros + sections - 1
    grad_ref, cots, dus, sent = refs[0], refs[1 : 1 + spans], refs[1 + spans : 1 + 2 * spans], refs[1 + 2 * spans :]
    rows, wide = dus[0].shape
    quarters = len(sent)
    width = cots[0].shape[1] // quarters
    section = where_ref[0]
    for m in range(micros):
        cot = grad_ref[m] if fresh else cots[m][...]
        du = dus[m][...]
        for s in range(sections - 1):
            at = m + sections - 1 - s
            cot = jnp.where(section == s, cots[at][...], cot)
            du = jnp.where(section == s, dus[at][...], du)
        where = slice(m * rows, (m + 1) * rows)
        for d, out_ref in enumerate(sent):
            out_ref[where, :width] = chosen_quarter(cot, where_ref[1] ^ d, quarters)
            out_ref[where, width : width + wide] = du
    for out_ref in sent:
        out_ref[:, width + wide :] = low_ref[...]


def grads_kernel(block, *refs):
    out_ref = refs[-1]
    quarters = len(refs) // 2
    xns = refs[quarters:-1]
    tokens, width = refs[0].shape[0], xns[0].shape[1]
    ranks, combos = out_ref.shape[0], out_ref.shape[1] // 2
    wide = ranks * combos
    xn = jnp.concatenate([ref[block * tokens : (block + 1) * tokens, :] for ref in xns])
    mixed = jnp.concatenate([ref[...] for ref in refs[:quarters]])
    dy = mixed[:, :width]
    du = mixed[:, width : width + wide]
    low = mixed[:, width + wide :]
    grad_a = lax.dot_general(du, xn, FIRST, preferred_element_type=f32)
    out_ref[:, :combos, :] = grad_a.astype(bf16).reshape(ranks, combos, width)
    grad_b = lax.dot_general(low, dy, FIRST, preferred_element_type=f32)
    out_ref[:, combos:, :] = grad_b.astype(bf16).reshape(ranks, combos, width)


def generate_kernel(cond_ref, down_ref, up_ref, out_ref):
    blocks, _, combos, _ = out_ref.shape
    cond = cond_ref[...]
    first = cond.astype(bf16)
    rest = cond - first.astype(f32)
    second = rest.astype(bf16)
    third = (rest - second.astype(f32)).astype(bf16)
    parts = jnp.concatenate([first, second, third])
    rows = cond.shape[0]
    for which, gen_ref in enumerate((down_ref, up_ref)):
        made = jnp.dot(parts, gen_ref[...], preferred_element_type=f32)
        made = made[:rows] + (made[rows : 2 * rows] + made[2 * rows :])
        out_ref[:, which] = made.astype(bf16).reshape(blocks, combos, -1)


def call(kernel, out_shape, operands, flops, moved):
    scalars = 1 if operands[0].dtype == jnp.int32 else 0
    return pl.pallas_call(
        kernel,
        out_shape=out_shape,
        in_specs=[SMEM] * scalars + [VMEM] * (len(operands) - scalars),
        out_specs=jax.tree.map(lambda _: VMEM, out_shape),
        compiler_params=pltpu.CompilerParams(vmem_limit_bytes=VMEM_LIMIT),
        cost_estimate=pl.CostEstimate(flops=flops, bytes_accessed=moved, transcendentals=0),
    )(*operands)


def swapped(parts, axes):
    count = lax.axis_size(axes)
    return [parts[0]] + [
        lax.ppermute(parts[d], axes, [(i, i ^ d) for i in range(count)])
        for d in range(1, count)
    ]


def from_sections(part):
    count = lax.axis_size("s")
    got = [part] + [
        lax.ppermute(part, "s", [((i + d) % count, i) for i in range(count)])
        for d in range(1, count)
    ]
    me = lax.axis_index("s")
    return jnp.stack([lax.select_n(lax.rem(i + count - me, count), *got) for i in range(count)])


def on_device(
    hidden_in, out_grad, gate_probs, expert_ids, task_ids, task_embed, slot_embed, gen_down, gen_up
):
    high = lax.Precision.HIGHEST
    sections = lax.axis_size("s")
    section_id = lax.axis_index("s")
    quarters = lax.axis_size(QUARTERS)
    ranks = lax.axis_size(RANKS)
    blocks, _, micros, rows, model = hidden_in.shape
    tasks, cond_width = task_embed.shape
    experts = slot_embed.shape[2]
    combos = tasks * experts
    width = model // quarters
    wide = ranks * combos
    items = blocks * micros
    tokens = micros * rows
    where = jnp.stack([section_id, lax.axis_index(QUARTERS)]).astype(jnp.int32)

    def shaped(*shape, dtype=bf16):
        return jax.ShapeDtypeStruct(shape, dtype)

    pre = task_embed[None, :, None, :] + slot_embed[:, 0][:, None, :, :]
    cond = jax.nn.silu(pre).reshape(blocks, combos, cond_width)
    mine = call(
        generate_kernel,
        shaped(blocks, 2, combos, width),
        (cond.reshape(blocks * combos, cond_width), gen_down, gen_up),
        12 * blocks * combos * cond_width * width,
        5 << 18,
    )
    filled = lax.all_gather(mine.reshape(blocks * 2 * combos, width), DP, axis=0, tiled=True)

    slots = from_sections(slot_embed[:, 0])
    x_items = hidden_in[:, 0].reshape(items, rows, model)
    normed, inv_items, *sent = call(
        prep_kernel,
        [shaped(items * rows, model), shaped(items, rows, 128, dtype=f32)]
        + [shaped(items * rows, width)] * quarters,
        (where, x_items),
        8 * items * rows * model,
        3 << 20,
    )
    normed_quarter = swapped(sent, QUARTERS)
    lane = jnp.arange(wide, dtype=jnp.int32)
    expert_of, task_of = lane % experts, (lane // experts) % tasks
    ids, gates = expert_ids[:, 0], gate_probs[:, 0]
    weights = jnp.where(ids[..., 0:1] == expert_of, gates[..., 0:1], 0.0) + jnp.where(
        ids[..., 1:2] == expert_of, gates[..., 1:2], 0.0
    )
    weights = jnp.where(task_ids[None, :, :, None] == task_of, weights, 0.0)
    weights_items = weights.reshape(items, rows, wide)

    filled, slots, normed, inv_items, normed_quarter, weights_items = lax.optimization_barrier(
        (filled, slots, normed, inv_items, normed_quarter, weights_items)
    )
    adapters = filled.reshape(ranks, quarters, blocks, 2, combos, width)
    adapters = [adapters[:, :, j] for j in range(blocks)]
    pairs = [(i, (i - 1) % sections) for i in range(sections)]
    last = items + sections - 2

    def low_of(block):
        return call(
            functools.partial(low_kernel, block),
            shaped(tokens, wide),
            (normed, weights_items.reshape(blocks * tokens, wide), adapters[block]),
            2 * tokens * wide * model,
            3 << 20,
        )

    def exchanged(block, low):
        span = slice((blocks - 1 - block) * micros, (blocks - block) * micros + sections - 1)
        fresh = block == blocks - 1
        cots = [out_grad[0] if cot is None else cot for cot in incoming[span]]
        parts = call(
            functools.partial(pack_kernel, micros, sections, fresh),
            [shaped(tokens, width + 2 * wide)] * quarters,
            (where, low, out_grad, *cots, *dus[span]),
            0,
            3 << 20,
        )
        return swapped(parts, QUARTERS)

    def partial_grads(block, mixed):
        return call(
            functools.partial(grads_kernel, block),
            shaped(ranks, 2 * combos, width),
            (*mixed, *normed_quarter),
            4 * quarters * tokens * wide * width,
            5 << 20,
        )

    def summed(got):
        scale = 1.0 / (micros * rows * lax.axis_size(DP))
        return (jnp.sum(got.astype(f32), axis=0) * scale).astype(bf16)

    def rank_rows(part):
        part = part.reshape(lax.axis_size("x"), -1, *part.shape[1:])
        got = lax.all_to_all(part, "x", 0, 0)
        part = jnp.sum(got.astype(f32), axis=0).astype(bf16)
        return lax.all_to_all(part, "zh", 0, 0)

    incoming, dus, results = [None], [], []
    for tick in range(last + 1):
        operands = [where]
        if tick < micros:
            operands.append(out_grad)
        if tick:
            operands.append(incoming[tick])
        if tick < micros:
            used = [adapters[1]]
        elif tick >= micros + sections - 1:
            used = [adapters[0]]
        else:
            used = [adapters[1], adapters[0]]
        result, du = call(
            functools.partial(tick_kernel, tick, sections, micros),
            [shaped(rows, model), shaped(rows, wide)],
            (*operands, x_items, inv_items, weights_items, *used),
            4 * rows * wide * model,
            5 << 20,
        )
        results.append(result)
        dus.append(du)
        if tick == last:
            break
        arriving = lax.ppermute(result, "s", pairs)
        if tick == 1:
            low_first = low_of(1)
            arriving, low_first = lax.optimization_barrier((arriving, low_first))
        if tick == 4:
            low_second = low_of(0)
            arriving, low_second = lax.optimization_barrier((arriving, low_second))
        if tick == micros + sections - 2:
            mixed = exchanged(1, low_first)
        if tick == micros + sections - 1:
            early = partial_grads(1, mixed)
            arriving, early = lax.optimization_barrier((arriving, early))
            early_got = lax.all_to_all(early, RANKS, 0, 0)
        incoming.append(arriving)
    mixed = exchanged(0, low_second)
    mixed[0], early_got = lax.optimization_barrier((mixed[0], early_got))
    late_got = rank_rows(partial_grads(0, mixed))

    hidden_out = jnp.stack(
        [
            lax.select_n(
                section_id,
                *[results[micros + m + sections - 1 - s] for s in range(sections)],
            )
            for m in range(micros)
        ]
    )
    hidden_out, late_got = lax.optimization_barrier((hidden_out, late_got))
    reduced = jnp.stack([summed(late_got), summed(early_got)])
    pre_all = task_embed[None, None, :, None, :] + slots[:, :, None, :, :]
    cond_all = jax.nn.silu(pre_all).reshape(sections * blocks * combos, cond_width)
    grads = from_sections(reduced).reshape(sections * blocks, 2, combos, width)
    grad_a = grads[:, 0].reshape(-1, width)
    grad_b = grads[:, 1].reshape(-1, width)
    d_cond = jnp.einsum("nf,wf->nw", grad_a, gen_down, preferred_element_type=f32)
    d_cond = d_cond + jnp.einsum("nf,wf->nw", grad_b, gen_up, preferred_element_type=f32)
    gate = jax.nn.sigmoid(pre_all)
    d_pre = d_cond.reshape(pre_all.shape) * gate * (1.0 + pre_all * (1.0 - gate))
    own = lax.dynamic_index_in_dim(d_pre, section_id, 0, keepdims=False)
    d_slot = jnp.sum(own, axis=1).reshape(blocks * experts, cond_width)
    d_task = jnp.sum(d_pre, axis=(0, 1, 3))
    small = jnp.concatenate([d_slot, d_task])
    held = small.reshape(-1, 128)
    held = jnp.pad(held, ((0, -held.shape[0] % 8), (0, 0)))
    got = lax.all_gather(held, QUARTERS, axis=0, tiled=True)
    held = jnp.sum(got.reshape(-1, *held.shape), axis=0)
    held = jnp.broadcast_to(held[None], (ranks, *held.shape))
    held = jnp.sum(lax.all_to_all(held, RANKS, 0, 0), axis=0)
    small = held[: small.size // 128].reshape(small.shape)
    d_slot = small[: blocks * experts].reshape(blocks, 1, experts, cond_width)
    d_task = small[blocks * experts :]
    d_gen_down = jnp.einsum("nw,nf->wf", cond_all, grad_a.astype(f32), precision=high)
    d_gen_up = jnp.einsum("nw,nf->wf", cond_all, grad_b.astype(f32), precision=high)
    return (hidden_out[None], d_gen_down, d_gen_up, d_task, d_slot)


def solution(mesh):
    split = Mesh(mesh.devices.reshape(mesh.devices.shape[0], 4, 4, 2, 2), AXES)
    placed = (
        P(None, "s", None, DP, None),
        P(None, DP, None),
        P(None, "s", None, DP, None),
        P(None, "s", None, DP, None),
        P(None, DP),
        P(),
        P(None, "s", None, None),
        P(None, DP),
        P(None, DP),
    )
    return jax.shard_map(
        on_device,
        mesh=split,
        in_specs=placed,
        out_specs=(
            P("s", None, DP, None),
            P(None, DP),
            P(None, DP),
            P(),
            P(None, "s", None, None),
        ),
        check_vma=False,
    )
```

```python
import functools

import jax
import jax.numpy as jnp
from jax import lax
from jax.experimental import pallas as pl
from jax.experimental.pallas import tpu as pltpu
from jax.sharding import Mesh, PartitionSpec as P

eps = 1e-05
bf16 = jnp.bfloat16
f32 = jnp.float32

AXES = ("s", "x", "zh", "zl", "c")
DP = ("x", "zh", "zl", "c")
RANKS = ("x", "zh")
QUARTERS = ("zl", "c")
VMEM = pl.BlockSpec(memory_space=pltpu.VMEM)
SMEM = pl.BlockSpec(memory_space=pltpu.SMEM)
LAST = (((1,), (1,)), ((), ()))
FIRST = (((0,), (0,)), ((), ()))
VMEM_LIMIT = 4 * 1024 * 1024


def adapter_rows(g_ref, which, q):
    part = g_ref[:, q, which]
    return part.reshape(part.shape[0] * part.shape[1], part.shape[2])


def chosen_quarter(value, index, quarters):
    width = value.shape[1] // quarters
    part = value[:, :width]
    for q in range(1, quarters):
        part = jnp.where(index == q, value[:, q * width : (q + 1) * width], part)
    return part


def prep_kernel(where_ref, x_ref, xn_ref, inv_ref, *sent):
    items, rows, _ = x_ref.shape
    for item in range(items):
        values = x_ref[item].astype(f32)
        inv = lax.rsqrt(jnp.mean(values * values, axis=1, keepdims=True) + eps)
        inv_ref[item] = jnp.broadcast_to(inv, (rows, inv_ref.shape[2]))
        normed = (values * inv).astype(bf16)
        where = slice(item * rows, (item + 1) * rows)
        xn_ref[where, :] = normed
        for d, out_ref in enumerate(sent):
            out_ref[where, :] = chosen_quarter(normed, where_ref[1] ^ d, len(sent))


def low_kernel(block, xn_ref, weights_ref, g_ref, out_ref):
    tokens, _ = out_ref.shape
    quarters, width = g_ref.shape[1], g_ref.shape[4]
    low = jnp.zeros(out_ref.shape, f32)
    for q in range(quarters):
        low += lax.dot_general(
            xn_ref[block * tokens : (block + 1) * tokens, q * width : (q + 1) * width],
            adapter_rows(g_ref, 0, q),
            LAST,
            preferred_element_type=f32,
        )
    weights = weights_ref[block * tokens : (block + 1) * tokens, :]
    out_ref[...] = (weights * low).astype(bf16)


def tick_kernel(tick, sections, micros, where_ref, *refs):
    refs = list(refs)
    section = where_ref[0]
    if tick < micros:
        grad = refs.pop(0)[tick]
        if tick:
            cot = jnp.where(section == sections - 1, grad, refs.pop(0)[...])
        else:
            cot = grad
    else:
        cot = refs.pop(0)[...]
    x_ref, inv_ref, weights_ref = refs[:3]
    dx_ref, du_ref = refs[-2:]
    adapters = refs[3:-2]
    position = jnp.clip(tick - (sections - 1 - section), 0, x_ref.shape[0] - 1)

    def layer(block, g_ref, item):
        quarters, width = g_ref.shape[1], g_ref.shape[4]
        back = jnp.zeros(du_ref.shape, f32)
        for q in range(quarters):
            back += lax.dot_general(
                cot[:, q * width : (q + 1) * width],
                adapter_rows(g_ref, 1, q),
                LAST,
                preferred_element_type=f32,
            )
        du = (weights_ref[item] * back).astype(bf16)
        du_ref[...] = du
        inv = inv_ref[item][:, :1]
        dxn, xf = [], []
        total = jnp.zeros((du.shape[0], 1), f32)
        for q in range(quarters):
            xf.append(x_ref[item, :, q * width : (q + 1) * width].astype(f32) * inv)
            dxn.append(jnp.dot(du, adapter_rows(g_ref, 0, q), preferred_element_type=f32))
            total += jnp.sum(dxn[q] * xf[q], axis=1, keepdims=True)
        mean = total * (1.0 / (quarters * width))
        for q in range(quarters):
            cols = slice(q * width, (q + 1) * width)
            dx_ref[:, cols] = (
                cot[:, cols].astype(f32) + inv * (dxn[q] - xf[q] * mean)
            ).astype(bf16)

    if tick < micros:
        layer(1, adapters[0], micros + position)
    elif tick >= micros + sections - 1:
        layer(0, adapters[0], position - micros)
    else:
        pl.when(position < micros)(lambda: layer(1, adapters[0], micros + position))
        pl.when(position >= micros)(lambda: layer(0, adapters[1], position - micros))


def pack_kernel(micros, sections, fresh, where_ref, *refs):
    spans = micros + sections - 1
    lows = refs[:2] if fresh else ()
    refs = refs[len(lows) :]
    grad_ref, cots, dus, sent = refs[0], refs[1 : 1 + spans], refs[1 + spans : 1 + 2 * spans], refs[1 + 2 * spans :]
    rows, wide = dus[0].shape
    quarters = len(sent)
    width = cots[0].shape[1] // quarters
    section = where_ref[0]
    for m in range(micros):
        cot = grad_ref[m] if fresh else cots[m][...]
        du = dus[m][...]
        for s in range(sections - 1):
            at = m + sections - 1 - s
            cot = jnp.where(section == s, cots[at][...], cot)
            du = jnp.where(section == s, dus[at][...], du)
        where = slice(m * rows, (m + 1) * rows)
        for d, out_ref in enumerate(sent):
            out_ref[where, :width] = chosen_quarter(cot, where_ref[1] ^ d, quarters)
            out_ref[where, width : width + wide] = du
    for out_ref in sent:
        for i, low_ref in enumerate(lows):
            out_ref[:, width + (1 + i) * wide : width + (2 + i) * wide] = low_ref[...]


def grads_kernel(block, low_at, *refs):
    out_ref = refs[-1]
    quarters = len(refs) // 3
    lows, xns = refs[quarters : 2 * quarters], refs[2 * quarters : -1]
    tokens, width = refs[0].shape[0], xns[0].shape[1]
    ranks, combos = out_ref.shape[0], out_ref.shape[1] // 2
    wide = ranks * combos
    xn = jnp.concatenate([ref[block * tokens : (block + 1) * tokens, :] for ref in xns])
    mixed = jnp.concatenate([ref[:, : width + wide] for ref in refs[:quarters]])
    dy = mixed[:, :width]
    du = mixed[:, width : width + wide]
    low = jnp.concatenate([ref[:, low_at : low_at + wide] for ref in lows])
    grad_a = lax.dot_general(du, xn, FIRST, preferred_element_type=f32)
    out_ref[:, :combos, :] = grad_a.astype(bf16).reshape(ranks, combos, width)
    grad_b = lax.dot_general(low, dy, FIRST, preferred_element_type=f32)
    out_ref[:, combos:, :] = grad_b.astype(bf16).reshape(ranks, combos, width)


def generate_kernel(task_ref, slot_ref, down_ref, up_ref, out_ref):
    blocks, _, combos, _ = out_ref.shape
    pre = jnp.concatenate(
        [
            slot_ref[j] + task_ref[t : t + 1, :]
            for j in range(blocks)
            for t in range(task_ref.shape[0])
        ]
    )
    cond = pre / (1.0 + jnp.exp(-pre))
    first = cond.astype(bf16)
    rest = cond - first.astype(f32)
    second = rest.astype(bf16)
    third = (rest - second.astype(f32)).astype(bf16)
    parts = jnp.concatenate([first, second, third])
    rows = cond.shape[0]
    for which, gen_ref in enumerate((down_ref, up_ref)):
        made = jnp.dot(parts, gen_ref[...], preferred_element_type=f32)
        made = made[:rows] + (made[rows : 2 * rows] + made[2 * rows :])
        out_ref[:, which] = made.astype(bf16).reshape(blocks, combos, -1)


def call(kernel, out_shape, operands, flops, moved):
    scalars = 1 if operands[0].dtype == jnp.int32 else 0
    return pl.pallas_call(
        kernel,
        out_shape=out_shape,
        in_specs=[SMEM] * scalars + [VMEM] * (len(operands) - scalars),
        out_specs=jax.tree.map(lambda _: VMEM, out_shape),
        compiler_params=pltpu.CompilerParams(vmem_limit_bytes=VMEM_LIMIT),
        cost_estimate=pl.CostEstimate(flops=flops, bytes_accessed=moved, transcendentals=0),
    )(*operands)


def swapped(parts, axes):
    count = lax.axis_size(axes)
    return [parts[0]] + [
        lax.ppermute(parts[d], axes, [(i, i ^ d) for i in range(count)])
        for d in range(1, count)
    ]


def from_sections(part):
    count = lax.axis_size("s")
    got = [part] + [
        lax.ppermute(part, "s", [((i + d) % count, i) for i in range(count)])
        for d in range(1, count)
    ]
    me = lax.axis_index("s")
    return jnp.stack([lax.select_n(lax.rem(i + count - me, count), *got) for i in range(count)])


def on_device(
    hidden_in, out_grad, gate_probs, expert_ids, task_ids, task_embed, slot_embed, gen_down, gen_up
):
    high = lax.Precision.HIGHEST
    sections = lax.axis_size("s")
    section_id = lax.axis_index("s")
    quarters = lax.axis_size(QUARTERS)
    ranks = lax.axis_size(RANKS)
    blocks, _, micros, rows, model = hidden_in.shape
    tasks, cond_width = task_embed.shape
    experts = slot_embed.shape[2]
    combos = tasks * experts
    width = model // quarters
    wide = ranks * combos
    items = blocks * micros
    tokens = micros * rows
    where = jnp.stack([section_id, lax.axis_index(QUARTERS)]).astype(jnp.int32)

    def shaped(*shape, dtype=bf16):
        return jax.ShapeDtypeStruct(shape, dtype)

    mine = call(
        generate_kernel,
        shaped(blocks, 2, combos, width),
        (task_embed, slot_embed[:, 0], gen_down, gen_up),
        12 * blocks * combos * cond_width * width,
        5 << 18,
    )
    filled = lax.all_gather(mine.reshape(blocks * 2 * combos, width), DP, axis=0, tiled=True)

    slots = from_sections(slot_embed[:, 0])
    x_items = hidden_in[:, 0].reshape(items, rows, model)
    normed, inv_items, *sent = call(
        prep_kernel,
        [shaped(items * rows, model), shaped(items, rows, 128, dtype=f32)]
        + [shaped(items * rows, width)] * quarters,
        (where, x_items),
        8 * items * rows * model,
        3 << 20,
    )
    normed_quarter = swapped(sent, QUARTERS)
    lane = jnp.arange(wide, dtype=jnp.int32)
    expert_of, task_of = lane % experts, (lane // experts) % tasks
    ids, gates = expert_ids[:, 0], gate_probs[:, 0]
    weights = jnp.where(ids[..., 0:1] == expert_of, gates[..., 0:1], 0.0) + jnp.where(
        ids[..., 1:2] == expert_of, gates[..., 1:2], 0.0
    )
    weights = jnp.where(task_ids[None, :, :, None] == task_of, weights, 0.0)
    weights_items = weights.reshape(items, rows, wide)

    filled, slots, normed, inv_items, normed_quarter, weights_items = lax.optimization_barrier(
        (filled, slots, normed, inv_items, normed_quarter, weights_items)
    )
    adapters = filled.reshape(ranks, quarters, blocks, 2, combos, width)
    adapters = [adapters, adapters[:, :, 1]]
    pairs = [(i, (i - 1) % sections) for i in range(sections)]
    last = items + sections - 2

    def low_of(block):
        return call(
            functools.partial(low_kernel, block),
            shaped(tokens, wide),
            (normed, weights_items.reshape(blocks * tokens, wide), adapters[block]),
            2 * tokens * wide * model,
            3 << 20,
        )

    def exchanged(block, *lows):
        span = slice((blocks - 1 - block) * micros, (blocks - block) * micros + sections - 1)
        fresh = block == blocks - 1
        cots = [out_grad[0] if cot is None else cot for cot in incoming[span]]
        parts = call(
            functools.partial(pack_kernel, micros, sections, fresh),
            [shaped(tokens, width + (1 + len(lows)) * wide)] * quarters,
            (where, *lows, out_grad, *cots, *dus[span]),
            0,
            3 << 20,
        )
        return swapped(parts, QUARTERS)

    def partial_grads(block, mixed, lows):
        return call(
            functools.partial(grads_kernel, block, width + (2 - block) * wide),
            shaped(ranks, 2 * combos, width),
            (*mixed, *lows, *normed_quarter),
            4 * quarters * tokens * wide * width,
            5 << 20,
        )

    incoming, dus, results = [None], [], []
    for tick in range(last + 1):
        operands = [where]
        if tick < micros:
            operands.append(out_grad)
        if tick:
            operands.append(incoming[tick])
        if tick < micros:
            used = [adapters[1]]
        elif tick >= micros + sections - 1:
            used = [adapters[0]]
        else:
            used = [adapters[1], adapters[0]]
        result, du = call(
            functools.partial(tick_kernel, tick, sections, micros),
            [shaped(rows, model), shaped(rows, wide)],
            (*operands, x_items, inv_items, weights_items, *used),
            4 * rows * wide * model,
            5 << 20,
        )
        results.append(result)
        dus.append(du)
        if tick == last:
            break
        arriving = lax.ppermute(result, "s", pairs)
        if tick == 1:
            low_first = low_of(1)
            arriving, low_first = lax.optimization_barrier((arriving, low_first))
        if tick == 2:
            whole, arriving = lax.optimization_barrier((adapters[0], arriving))
            adapters[0] = whole[:, :, 0]
        if tick == 4:
            low_second = low_of(0)
            arriving, low_second = lax.optimization_barrier((arriving, low_second))
        if tick == micros + sections - 2:
            first = exchanged(1, low_first, low_second)
        if tick == micros + sections:
            early = partial_grads(1, first, first)
            arriving, early = lax.optimization_barrier((arriving, early))
            early = lax.psum_scatter(early, RANKS, scatter_dimension=0)
        incoming.append(arriving)
    part = partial_grads(0, exchanged(0), first)
    part = part.reshape(lax.axis_size("x"), -1, 2 * combos, width)
    part = lax.all_to_all(part, "x", 0, 0)
    part = jnp.sum(part.astype(f32), axis=0).astype(bf16)
    part = lax.all_to_all(part, "zh", 0, 0)
    scale = 1.0 / (micros * rows * lax.axis_size(DP))
    early = from_sections((early.astype(f32) * scale).astype(bf16))

    hidden_out = jnp.stack(
        [
            lax.select_n(
                section_id,
                *[results[micros + m + sections - 1 - s] for s in range(sections)],
            )
            for m in range(micros)
        ]
    )
    hidden_out, part, early = lax.optimization_barrier((hidden_out, part, early))
    late = from_sections((jnp.sum(part.astype(f32), axis=0) * scale).astype(bf16))
    pre_all = task_embed[None, None, :, None, :] + slots.swapaxes(0, 1)[:, :, None, :, :]
    cond_all = jax.nn.silu(pre_all).reshape(sections * blocks * combos, cond_width)
    grads = jnp.stack([late, early]).reshape(sections * blocks, 2, combos, width)
    grad_a = grads[:, 0].reshape(-1, width)
    grad_b = grads[:, 1].reshape(-1, width)
    d_cond = jnp.einsum("nf,wf->nw", grad_a, gen_down, preferred_element_type=f32)
    d_cond = d_cond + jnp.einsum("nf,wf->nw", grad_b, gen_up, preferred_element_type=f32)
    gate = jax.nn.sigmoid(pre_all)
    d_pre = d_cond.reshape(pre_all.shape) * gate * (1.0 + pre_all * (1.0 - gate))
    own = lax.dynamic_index_in_dim(d_pre, section_id, 1, keepdims=False)
    d_slot = jnp.sum(own, axis=1).reshape(blocks * experts, cond_width)
    d_task = jnp.sum(d_pre, axis=(0, 1, 3))
    small = jnp.concatenate([d_slot, d_task])
    held = small.reshape(-1, 128)
    held = jnp.pad(held, ((0, -held.shape[0] % 8), (0, 0)))
    got = lax.all_gather(held, QUARTERS, axis=0, tiled=True)
    held = jnp.sum(got.reshape(-1, *held.shape), axis=0)
    held = jnp.broadcast_to(held[None], (ranks, *held.shape))
    held = jnp.sum(lax.all_to_all(held, RANKS, 0, 0), axis=0)
    small = held[: small.size // 128].reshape(small.shape)
    d_slot = small[: blocks * experts].reshape(blocks, 1, experts, cond_width)
    d_task = small[blocks * experts :]
    d_gen_down = jnp.einsum("nw,nf->wf", cond_all, grad_a.astype(f32), precision=high)
    d_gen_up = jnp.einsum("nw,nf->wf", cond_all, grad_b.astype(f32), precision=high)
    return (hidden_out[None], d_gen_down, d_gen_up, d_task, d_slot)


def solution(mesh):
    split = Mesh(mesh.devices.reshape(mesh.devices.shape[0], 4, 4, 2, 2), AXES)
    placed = (
        P(None, "s", None, DP, None),
        P(None, DP, None),
        P(None, "s", None, DP, None),
        P(None, "s", None, DP, None),
        P(None, DP),
        P(),
        P(None, "s", None, None),
        P(None, DP),
        P(None, DP),
    )
    return jax.shard_map(
        on_device,
        mesh=split,
        in_specs=placed,
        out_specs=(
            P("s", None, DP, None),
            P(None, DP),
            P(None, DP),
            P(),
            P(None, "s", None, None),
        ),
        check_vma=False,
    )
```

```python
import functools

import jax
import jax.numpy as jnp
from jax import lax
from jax.experimental import pallas as pl
from jax.experimental.pallas import tpu as pltpu
from jax.sharding import Mesh, PartitionSpec as P

eps = 1e-05
bf16 = jnp.bfloat16
f32 = jnp.float32

AXES = ("s", "x", "zh", "zl", "c")
DP = ("x", "zh", "zl", "c")
RANKS = ("x", "zh")
QUARTERS = ("zl", "c")
VMEM = pl.BlockSpec(memory_space=pltpu.VMEM)
SMEM = pl.BlockSpec(memory_space=pltpu.SMEM)
LAST = (((1,), (1,)), ((), ()))
FIRST = (((0,), (0,)), ((), ()))
VMEM_LIMIT = 4 * 1024 * 1024
HOP = 2


def adapter_rows(g_ref, which, q):
    part = g_ref[:, q, which]
    return part.reshape(part.shape[0] * part.shape[1], part.shape[2])


def chosen_quarter(value, index, quarters):
    width = value.shape[1] // quarters
    part = value[:, :width]
    for q in range(1, quarters):
        part = jnp.where(index == q, value[:, q * width : (q + 1) * width], part)
    return part


def prep_kernel(where_ref, x_ref, xn_ref, inv_ref, *sent):
    items, rows, _ = x_ref.shape
    for item in range(items):
        values = x_ref[item].astype(f32)
        inv = lax.rsqrt(jnp.mean(values * values, axis=1, keepdims=True) + eps)
        inv_ref[item] = jnp.broadcast_to(inv, (rows, inv_ref.shape[2]))
        normed = (values * inv).astype(bf16)
        where = slice(item * rows, (item + 1) * rows)
        xn_ref[where, :] = normed
        for d, out_ref in enumerate(sent):
            out_ref[where, :] = chosen_quarter(normed, where_ref[1] ^ d, len(sent))


def low_kernel(block, xn_ref, weights_ref, g_ref, out_ref):
    tokens, _ = out_ref.shape
    quarters, width = g_ref.shape[1], g_ref.shape[4]
    low = jnp.zeros(out_ref.shape, f32)
    for q in range(quarters):
        low += lax.dot_general(
            xn_ref[block * tokens : (block + 1) * tokens, q * width : (q + 1) * width],
            adapter_rows(g_ref, 0, q),
            LAST,
            preferred_element_type=f32,
        )
    weights = weights_ref[block * tokens : (block + 1) * tokens, :]
    out_ref[...] = (weights * low).astype(bf16)


def tick_kernel(tick, sections, micros, where_ref, *refs):
    refs = list(refs)
    section = where_ref[0]
    if tick < micros:
        grad = refs.pop(0)[tick]
        if tick >= HOP:
            cot = jnp.where(section == sections - 1, grad, refs.pop(0)[...])
        else:
            cot = grad
    else:
        cot = refs.pop(0)[...]
    x_ref, inv_ref, weights_ref = refs[:3]
    dx_ref, du_ref = refs[-2:]
    adapters = refs[3:-2]
    position = tick - HOP * (sections - 1 - section)
    second = position - HOP * sections
    first_item = micros + jnp.clip(position, 0, micros - 1)
    second_item = jnp.clip(second, 0, micros - 1)

    def layer(g_ref, item):
        quarters, width = g_ref.shape[1], g_ref.shape[4]
        back = jnp.zeros(du_ref.shape, f32)
        for q in range(quarters):
            back += lax.dot_general(
                cot[:, q * width : (q + 1) * width],
                adapter_rows(g_ref, 1, q),
                LAST,
                preferred_element_type=f32,
            )
        du = (weights_ref[item] * back).astype(bf16)
        du_ref[...] = du
        inv = inv_ref[item][:, :1]
        dxn, xf = [], []
        total = jnp.zeros((du.shape[0], 1), f32)
        for q in range(quarters):
            xf.append(x_ref[item, :, q * width : (q + 1) * width].astype(f32) * inv)
            dxn.append(jnp.dot(du, adapter_rows(g_ref, 0, q), preferred_element_type=f32))
            total += jnp.sum(dxn[q] * xf[q], axis=1, keepdims=True)
        mean = total * (1.0 / (quarters * width))
        for q in range(quarters):
            cols = slice(q * width, (q + 1) * width)
            dx_ref[:, cols] = (
                cot[:, cols].astype(f32) + inv * (dxn[q] - xf[q] * mean)
            ).astype(bf16)

    if tick < HOP * sections:
        layer(adapters[0], first_item)
    elif tick >= HOP * (sections - 1) + micros:
        layer(adapters[0], second_item)
    else:
        pl.when(second < 0)(lambda: layer(adapters[0], first_item))
        pl.when(second >= 0)(lambda: layer(adapters[1], second_item))


def pack_kernel(micros, sections, fresh, where_ref, *refs):
    spans = micros + HOP * (sections - 1)
    lows = refs[:2] if fresh else ()
    refs = refs[len(lows) :]
    grad_ref, cots, dus, sent = refs[0], refs[1 : 1 + spans], refs[1 + spans : 1 + 2 * spans], refs[1 + 2 * spans :]
    rows, wide = dus[0].shape
    quarters = len(sent)
    width = cots[0].shape[1] // quarters
    section = where_ref[0]
    for m in range(micros):
        cot = grad_ref[m] if fresh else cots[m][...]
        du = dus[m][...]
        for s in range(sections - 1):
            at = m + HOP * (sections - 1 - s)
            cot = jnp.where(section == s, cots[at][...], cot)
            du = jnp.where(section == s, dus[at][...], du)
        where = slice(m * rows, (m + 1) * rows)
        for d, out_ref in enumerate(sent):
            out_ref[where, :width] = chosen_quarter(cot, where_ref[1] ^ d, quarters)
            out_ref[where, width : width + wide] = du
    for out_ref in sent:
        for i, low_ref in enumerate(lows):
            out_ref[:, width + (1 + i) * wide : width + (2 + i) * wide] = low_ref[...]


def grads_kernel(block, low_at, *refs):
    out_ref = refs[-1]
    quarters = len(refs) // 3
    lows, xns = refs[quarters : 2 * quarters], refs[2 * quarters : -1]
    tokens, width = refs[0].shape[0], xns[0].shape[1]
    ranks, combos = out_ref.shape[0], out_ref.shape[1] // 2
    wide = ranks * combos
    xn = jnp.concatenate([ref[block * tokens : (block + 1) * tokens, :] for ref in xns])
    mixed = jnp.concatenate([ref[:, : width + wide] for ref in refs[:quarters]])
    dy = mixed[:, :width]
    du = mixed[:, width : width + wide]
    low = jnp.concatenate([ref[:, low_at : low_at + wide] for ref in lows])
    grad_a = lax.dot_general(du, xn, FIRST, preferred_element_type=f32)
    out_ref[:, :combos, :] = grad_a.astype(bf16).reshape(ranks, combos, width)
    grad_b = lax.dot_general(low, dy, FIRST, preferred_element_type=f32)
    out_ref[:, combos:, :] = grad_b.astype(bf16).reshape(ranks, combos, width)


def generate_kernel(task_ref, slot_ref, down_ref, up_ref, out_ref):
    blocks, _, combos, _ = out_ref.shape
    pre = jnp.concatenate(
        [
            slot_ref[j] + task_ref[t : t + 1, :]
            for j in range(blocks)
            for t in range(task_ref.shape[0])
        ]
    )
    cond = pre / (1.0 + jnp.exp(-pre))
    first = cond.astype(bf16)
    rest = cond - first.astype(f32)
    second = rest.astype(bf16)
    third = (rest - second.astype(f32)).astype(bf16)
    parts = jnp.concatenate([first, second, third])
    rows = cond.shape[0]
    for which, gen_ref in enumerate((down_ref, up_ref)):
        made = jnp.dot(parts, gen_ref[...], preferred_element_type=f32)
        made = made[:rows] + (made[rows : 2 * rows] + made[2 * rows :])
        out_ref[:, which] = made.astype(bf16).reshape(blocks, combos, -1)


def call(kernel, out_shape, operands, flops, moved):
    scalars = 1 if operands[0].dtype == jnp.int32 else 0
    return pl.pallas_call(
        kernel,
        out_shape=out_shape,
        in_specs=[SMEM] * scalars + [VMEM] * (len(operands) - scalars),
        out_specs=jax.tree.map(lambda _: VMEM, out_shape),
        compiler_params=pltpu.CompilerParams(vmem_limit_bytes=VMEM_LIMIT),
        cost_estimate=pl.CostEstimate(flops=flops, bytes_accessed=moved, transcendentals=0),
    )(*operands)


def swapped(parts, axes):
    count = lax.axis_size(axes)
    return [parts[0]] + [
        lax.ppermute(parts[d], axes, [(i, i ^ d) for i in range(count)])
        for d in range(1, count)
    ]


def from_sections(part):
    count = lax.axis_size("s")
    got = [part] + [
        lax.ppermute(part, "s", [((i + d) % count, i) for i in range(count)])
        for d in range(1, count)
    ]
    me = lax.axis_index("s")
    return jnp.stack([lax.select_n(lax.rem(i + count - me, count), *got) for i in range(count)])


def on_device(
    hidden_in, out_grad, gate_probs, expert_ids, task_ids, task_embed, slot_embed, gen_down, gen_up
):
    high = lax.Precision.HIGHEST
    sections = lax.axis_size("s")
    section_id = lax.axis_index("s")
    quarters = lax.axis_size(QUARTERS)
    ranks = lax.axis_size(RANKS)
    blocks, _, micros, rows, model = hidden_in.shape
    tasks, cond_width = task_embed.shape
    experts = slot_embed.shape[2]
    combos = tasks * experts
    width = model // quarters
    wide = ranks * combos
    items = blocks * micros
    tokens = micros * rows
    where = jnp.stack([section_id, lax.axis_index(QUARTERS)]).astype(jnp.int32)

    def shaped(*shape, dtype=bf16):
        return jax.ShapeDtypeStruct(shape, dtype)

    mine = call(
        generate_kernel,
        shaped(blocks, 2, combos, width),
        (task_embed, slot_embed[:, 0], gen_down, gen_up),
        12 * blocks * combos * cond_width * width,
        5 << 18,
    )
    filled = lax.all_gather(mine.reshape(blocks * 2 * combos, width), DP, axis=0, tiled=True)

    slots = from_sections(slot_embed[:, 0])
    x_items = hidden_in[:, 0].reshape(items, rows, model)
    normed, inv_items, *sent = call(
        prep_kernel,
        [shaped(items * rows, model), shaped(items, rows, 128, dtype=f32)]
        + [shaped(items * rows, width)] * quarters,
        (where, x_items),
        8 * items * rows * model,
        3 << 20,
    )
    normed_quarter = swapped(sent, QUARTERS)
    lane = jnp.arange(wide, dtype=jnp.int32)
    expert_of, task_of = lane % experts, (lane // experts) % tasks
    ids, gates = expert_ids[:, 0], gate_probs[:, 0]
    weights = jnp.where(ids[..., 0:1] == expert_of, gates[..., 0:1], 0.0) + jnp.where(
        ids[..., 1:2] == expert_of, gates[..., 1:2], 0.0
    )
    weights = jnp.where(task_ids[None, :, :, None] == task_of, weights, 0.0)
    weights_items = weights.reshape(items, rows, wide)

    filled, slots, normed, inv_items, normed_quarter, weights_items = lax.optimization_barrier(
        (filled, slots, normed, inv_items, normed_quarter, weights_items)
    )
    adapters = filled.reshape(ranks, quarters, blocks, 2, combos, width)
    adapters = [adapters, adapters[:, :, 1]]
    last = HOP * (2 * sections - 1) + micros - 1

    def active(tick, section):
        position = tick - HOP * (sections - 1 - section)
        if 0 <= position < micros:
            return 1
        return 0 if 0 <= position - HOP * sections < micros else None

    def low_of(block):
        return call(
            functools.partial(low_kernel, block),
            shaped(tokens, wide),
            (normed, weights_items.reshape(blocks * tokens, wide), adapters[block]),
            2 * tokens * wide * model,
            3 << 20,
        )

    def exchanged(block, *lows):
        start = 0 if block == 1 else HOP * sections
        span = slice(start, start + micros + HOP * (sections - 1))
        fresh = block == blocks - 1
        cots = [out_grad[0] if cot is None else cot for cot in incoming[span]]
        parts = call(
            functools.partial(pack_kernel, micros, sections, fresh),
            [shaped(tokens, width + (1 + len(lows)) * wide)] * quarters,
            (where, *lows, out_grad, *cots, *dus[span]),
            0,
            3 << 20,
        )
        return swapped(parts, QUARTERS)

    def partial_grads(block, mixed, lows):
        return call(
            functools.partial(grads_kernel, block, width + (2 - block) * wide),
            shaped(ranks, 2 * combos, width),
            (*mixed, *lows, *normed_quarter),
            4 * quarters * tokens * wide * width,
            5 << 20,
        )

    incoming, dus, results = [None] * HOP, [], []
    for tick in range(last + 1):
        operands = [where]
        if tick < micros:
            operands.append(out_grad)
        if tick >= HOP:
            incoming[tick], dus[-1] = lax.optimization_barrier((incoming[tick], dus[-1]))
            operands.append(incoming[tick])
        if tick < HOP * sections:
            used = [adapters[1]]
        elif tick >= HOP * (sections - 1) + micros:
            used = [adapters[0]]
        else:
            used = [adapters[1], adapters[0]]
        result, du = call(
            functools.partial(tick_kernel, tick, sections, micros),
            [shaped(rows, model), shaped(rows, wide)],
            (*operands, x_items, inv_items, weights_items, *used),
            4 * rows * wide * model,
            5 << 20,
        )
        results.append(result)
        dus.append(du)
        if tick > last - HOP:
            continue
        pairs = [
            (i, (i - 1) % sections)
            for i in range(sections)
            if active(tick, i) == 1 or (i and active(tick, i) == 0)
        ]
        arriving = lax.ppermute(result, "s", pairs)
        if tick == 1:
            low_first = low_of(1)
            arriving, low_first = lax.optimization_barrier((arriving, low_first))
        if tick == 3:
            whole, arriving = lax.optimization_barrier((adapters[0], arriving))
            adapters[0] = whole[:, :, 0]
        if tick == 6:
            low_second = low_of(0)
            arriving, low_second = lax.optimization_barrier((arriving, low_second))
        if tick == HOP * (sections - 1) + micros - 1:
            first = exchanged(1, low_first, low_second)
        if tick == HOP * (sections - 1) + micros + 1:
            early = partial_grads(1, first, first)
            arriving, early = lax.optimization_barrier((arriving, early))
            early = lax.all_to_all(early, RANKS, 0, 0)
        incoming.append(arriving)
    mixed = exchanged(0)
    mixed[0], early = lax.optimization_barrier((mixed[0], early))
    part = partial_grads(0, mixed, first)
    part = part.reshape(lax.axis_size("x"), -1, 2 * combos, width)
    part = lax.all_to_all(part, "x", 0, 0)
    part = jnp.sum(part.astype(f32), axis=0).astype(bf16)
    part = lax.all_to_all(part, "zh", 0, 0)
    scale = 1.0 / (micros * rows * lax.axis_size(DP))
    early = from_sections((jnp.sum(early.astype(f32), axis=0) * scale).astype(bf16))

    hidden_out = jnp.stack(
        [
            lax.select_n(
                section_id,
                *[results[m + HOP * (2 * sections - 1 - s)] for s in range(sections)],
            )
            for m in range(micros)
        ]
    )
    hidden_out, part, early = lax.optimization_barrier((hidden_out, part, early))
    late = from_sections((jnp.sum(part.astype(f32), axis=0) * scale).astype(bf16))
    pre_all = task_embed[None, None, :, None, :] + slots.swapaxes(0, 1)[:, :, None, :, :]
    cond_all = jax.nn.silu(pre_all).reshape(sections * blocks * combos, cond_width)
    grads = jnp.stack([late, early]).reshape(sections * blocks, 2, combos, width)
    grad_a = grads[:, 0].reshape(-1, width)
    grad_b = grads[:, 1].reshape(-1, width)
    d_cond = jnp.einsum("nf,wf->nw", grad_a, gen_down, preferred_element_type=f32)
    d_cond = d_cond + jnp.einsum("nf,wf->nw", grad_b, gen_up, preferred_element_type=f32)
    gate = jax.nn.sigmoid(pre_all)
    d_pre = d_cond.reshape(pre_all.shape) * gate * (1.0 + pre_all * (1.0 - gate))
    own = lax.dynamic_index_in_dim(d_pre, section_id, 1, keepdims=False)
    d_slot = jnp.sum(own, axis=1).reshape(blocks * experts, cond_width)
    d_task = jnp.sum(d_pre, axis=(0, 1, 3))
    small = jnp.concatenate([d_slot, d_task])
    held = small.reshape(-1, 128)
    held = jnp.pad(held, ((0, -held.shape[0] % 8), (0, 0)))
    got = lax.all_gather(held, QUARTERS, axis=0, tiled=True)
    held = jnp.sum(got.reshape(-1, *held.shape), axis=0)
    held = jnp.broadcast_to(held[None], (ranks, *held.shape))
    held = jnp.sum(lax.all_to_all(held, RANKS, 0, 0), axis=0)
    small = held[: small.size // 128].reshape(small.shape)
    d_slot = small[: blocks * experts].reshape(blocks, 1, experts, cond_width)
    d_task = small[blocks * experts :]
    d_gen_down = jnp.einsum("nw,nf->wf", cond_all, grad_a.astype(f32), precision=high)
    d_gen_up = jnp.einsum("nw,nf->wf", cond_all, grad_b.astype(f32), precision=high)
    return (hidden_out[None], d_gen_down, d_gen_up, d_task, d_slot)


def solution(mesh):
    split = Mesh(mesh.devices.reshape(mesh.devices.shape[0], 4, 4, 2, 2), AXES)
    placed = (
        P(None, "s", None, DP, None),
        P(None, DP, None),
        P(None, "s", None, DP, None),
        P(None, "s", None, DP, None),
        P(None, DP),
        P(),
        P(None, "s", None, None),
        P(None, DP),
        P(None, DP),
    )
    return jax.shard_map(
        on_device,
        mesh=split,
        in_specs=placed,
        out_specs=(
            P("s", None, DP, None),
            P(None, DP),
            P(None, DP),
            P(),
            P(None, "s", None, None),
        ),
        check_vma=False,
    )
```

```python
import functools

import jax
import jax.numpy as jnp
from jax import lax
from jax.experimental import pallas as pl
from jax.experimental.pallas import tpu as pltpu
from jax.sharding import Mesh, PartitionSpec as P

eps = 1e-05
bf16 = jnp.bfloat16
f32 = jnp.float32

AXES = ("s", "x", "zh", "zl", "c")
DP = ("x", "zh", "zl", "c")
RANKS = ("x", "zh")
QUARTERS = ("zl", "c")
VMEM = pl.BlockSpec(memory_space=pltpu.VMEM)
SMEM = pl.BlockSpec(memory_space=pltpu.SMEM)
LAST = (((1,), (1,)), ((), ()))
FIRST = (((0,), (0,)), ((), ()))
VMEM_LIMIT = 4 * 1024 * 1024
HOP = 1


def adapter_rows(g_ref, which, q):
    part = g_ref[:, q, which]
    return part.reshape(part.shape[0] * part.shape[1], part.shape[2])


def chosen_quarter(value, index, quarters):
    width = value.shape[1] // quarters
    part = value[:, :width]
    for q in range(1, quarters):
        part = jnp.where(index == q, value[:, q * width : (q + 1) * width], part)
    return part


def prep_kernel(where_ref, x_ref, xn_ref, inv_ref, *sent):
    items, rows, _ = x_ref.shape
    for item in range(items):
        values = x_ref[item].astype(f32)
        inv = lax.rsqrt(jnp.mean(values * values, axis=1, keepdims=True) + eps)
        inv_ref[item] = jnp.broadcast_to(inv, (rows, inv_ref.shape[2]))
        normed = (values * inv).astype(bf16)
        where = slice(item * rows, (item + 1) * rows)
        xn_ref[where, :] = normed
        for d, out_ref in enumerate(sent):
            out_ref[where, :] = chosen_quarter(normed, where_ref[1] ^ d, len(sent))


def low_kernel(block, xn_ref, weights_ref, g_ref, out_ref):
    tokens, _ = out_ref.shape
    quarters, width = g_ref.shape[1], g_ref.shape[4]
    low = jnp.zeros(out_ref.shape, f32)
    for q in range(quarters):
        low += lax.dot_general(
            xn_ref[block * tokens : (block + 1) * tokens, q * width : (q + 1) * width],
            adapter_rows(g_ref, 0, q),
            LAST,
            preferred_element_type=f32,
        )
    weights = weights_ref[block * tokens : (block + 1) * tokens, :]
    out_ref[...] = (weights * low).astype(bf16)


def tick_kernel(tick, sections, micros, where_ref, *refs):
    refs = list(refs)
    section = where_ref[0]
    if tick < micros:
        grad = refs.pop(0)[tick]
        if tick >= HOP:
            cot = jnp.where(section == sections - 1, grad, refs.pop(0)[...])
        else:
            cot = grad
    else:
        cot = refs.pop(0)[...]
    x_ref, inv_ref, weights_ref = refs[:3]
    dx_ref, du_ref = refs[-2:]
    adapters = refs[3:-2]
    position = tick - HOP * (sections - 1 - section)
    second = position - HOP * sections
    first_item = micros + jnp.clip(position, 0, micros - 1)
    second_item = jnp.clip(second, 0, micros - 1)

    def layer(g_ref, item):
        quarters, width = g_ref.shape[1], g_ref.shape[4]
        back = jnp.zeros(du_ref.shape, f32)
        for q in range(quarters):
            back += lax.dot_general(
                cot[:, q * width : (q + 1) * width],
                adapter_rows(g_ref, 1, q),
                LAST,
                preferred_element_type=f32,
            )
        du = (weights_ref[item] * back).astype(bf16)
        du_ref[...] = du
        inv = inv_ref[item][:, :1]
        dxn, xf = [], []
        total = jnp.zeros((du.shape[0], 1), f32)
        for q in range(quarters):
            xf.append(x_ref[item, :, q * width : (q + 1) * width].astype(f32) * inv)
            dxn.append(jnp.dot(du, adapter_rows(g_ref, 0, q), preferred_element_type=f32))
            total += jnp.sum(dxn[q] * xf[q], axis=1, keepdims=True)
        mean = total * (1.0 / (quarters * width))
        for q in range(quarters):
            cols = slice(q * width, (q + 1) * width)
            dx_ref[:, cols] = (
                cot[:, cols].astype(f32) + inv * (dxn[q] - xf[q] * mean)
            ).astype(bf16)

    if tick < HOP * sections:
        layer(adapters[0], first_item)
    elif tick >= HOP * (sections - 1) + micros:
        layer(adapters[0], second_item)
    else:
        pl.when(second < 0)(lambda: layer(adapters[0], first_item))
        pl.when(second >= 0)(lambda: layer(adapters[1], second_item))


def pack_kernel(micros, sections, fresh, where_ref, *refs):
    spans = micros + HOP * (sections - 1)
    lows = refs[:2] if fresh else ()
    refs = refs[len(lows) :]
    grad_ref, cots, dus, sent = refs[0], refs[1 : 1 + spans], refs[1 + spans : 1 + 2 * spans], refs[1 + 2 * spans :]
    rows, wide = dus[0].shape
    quarters = len(sent)
    width = cots[0].shape[1] // quarters
    section = where_ref[0]
    for m in range(micros):
        cot = grad_ref[m] if fresh else cots[m][...]
        du = dus[m][...]
        for s in range(sections - 1):
            at = m + HOP * (sections - 1 - s)
            cot = jnp.where(section == s, cots[at][...], cot)
            du = jnp.where(section == s, dus[at][...], du)
        where = slice(m * rows, (m + 1) * rows)
        for d, out_ref in enumerate(sent):
            out_ref[where, :width] = chosen_quarter(cot, where_ref[1] ^ d, quarters)
            out_ref[where, width : width + wide] = du
    for out_ref in sent:
        for i, low_ref in enumerate(lows):
            out_ref[:, width + (1 + i) * wide : width + (2 + i) * wide] = low_ref[...]


def grads_kernel(block, low_at, *refs):
    out_ref = refs[-1]
    quarters = len(refs) // 3
    lows, xns = refs[quarters : 2 * quarters], refs[2 * quarters : -1]
    tokens, width = refs[0].shape[0], xns[0].shape[1]
    ranks, combos = out_ref.shape[0], out_ref.shape[1] // 2
    wide = ranks * combos
    xn = jnp.concatenate([ref[block * tokens : (block + 1) * tokens, :] for ref in xns])
    mixed = jnp.concatenate([ref[:, : width + wide] for ref in refs[:quarters]])
    dy = mixed[:, :width]
    du = mixed[:, width : width + wide]
    low = jnp.concatenate([ref[:, low_at : low_at + wide] for ref in lows])
    grad_a = lax.dot_general(du, xn, FIRST, preferred_element_type=f32)
    out_ref[:, :combos, :] = grad_a.astype(bf16).reshape(ranks, combos, width)
    grad_b = lax.dot_general(low, dy, FIRST, preferred_element_type=f32)
    out_ref[:, combos:, :] = grad_b.astype(bf16).reshape(ranks, combos, width)


def generate_kernel(task_ref, slot_ref, down_ref, up_ref, out_ref):
    blocks, _, combos, _ = out_ref.shape
    pre = jnp.concatenate(
        [
            slot_ref[j] + task_ref[t : t + 1, :]
            for j in range(blocks)
            for t in range(task_ref.shape[0])
        ]
    )
    cond = pre / (1.0 + jnp.exp(-pre))
    first = cond.astype(bf16)
    rest = cond - first.astype(f32)
    second = rest.astype(bf16)
    third = (rest - second.astype(f32)).astype(bf16)
    parts = jnp.concatenate([first, second, third])
    rows = cond.shape[0]
    for which, gen_ref in enumerate((down_ref, up_ref)):
        made = jnp.dot(parts, gen_ref[...], preferred_element_type=f32)
        made = made[:rows] + (made[rows : 2 * rows] + made[2 * rows :])
        out_ref[:, which] = made.astype(bf16).reshape(blocks, combos, -1)


def call(kernel, out_shape, operands, flops, moved):
    scalars = 1 if operands[0].dtype == jnp.int32 else 0
    return pl.pallas_call(
        kernel,
        out_shape=out_shape,
        in_specs=[SMEM] * scalars + [VMEM] * (len(operands) - scalars),
        out_specs=jax.tree.map(lambda _: VMEM, out_shape),
        compiler_params=pltpu.CompilerParams(vmem_limit_bytes=VMEM_LIMIT),
        cost_estimate=pl.CostEstimate(flops=flops, bytes_accessed=moved, transcendentals=0),
    )(*operands)


def swapped(parts, axes):
    count = lax.axis_size(axes)
    return [parts[0]] + [
        lax.ppermute(parts[d], axes, [(i, i ^ d) for i in range(count)])
        for d in range(1, count)
    ]


def from_sections(part):
    count = lax.axis_size("s")
    got = [part] + [
        lax.ppermute(part, "s", [((i + d) % count, i) for i in range(count)])
        for d in range(1, count)
    ]
    me = lax.axis_index("s")
    return jnp.stack([lax.select_n(lax.rem(i + count - me, count), *got) for i in range(count)])


def on_device(
    hidden_in, out_grad, gate_probs, expert_ids, task_ids, task_embed, slot_embed, gen_down, gen_up
):
    high = lax.Precision.HIGHEST
    sections = lax.axis_size("s")
    section_id = lax.axis_index("s")
    quarters = lax.axis_size(QUARTERS)
    ranks = lax.axis_size(RANKS)
    blocks, _, micros, rows, model = hidden_in.shape
    tasks, cond_width = task_embed.shape
    experts = slot_embed.shape[2]
    combos = tasks * experts
    width = model // quarters
    wide = ranks * combos
    items = blocks * micros
    tokens = micros * rows
    where = jnp.stack([section_id, lax.axis_index(QUARTERS)]).astype(jnp.int32)

    def shaped(*shape, dtype=bf16):
        return jax.ShapeDtypeStruct(shape, dtype)

    mine = call(
        generate_kernel,
        shaped(blocks, 2, combos, width),
        (task_embed, slot_embed[:, 0], gen_down, gen_up),
        12 * blocks * combos * cond_width * width,
        5 << 18,
    )
    filled = lax.all_gather(mine.reshape(blocks * 2 * combos, width), DP, axis=0, tiled=True)

    slots = from_sections(slot_embed[:, 0])
    x_items = hidden_in[:, 0].reshape(items, rows, model)
    normed, inv_items, *sent = call(
        prep_kernel,
        [shaped(items * rows, model), shaped(items, rows, 128, dtype=f32)]
        + [shaped(items * rows, width)] * quarters,
        (where, x_items),
        8 * items * rows * model,
        3 << 20,
    )
    normed_quarter = swapped(sent, QUARTERS)
    lane = jnp.arange(wide, dtype=jnp.int32)
    expert_of, task_of = lane % experts, (lane // experts) % tasks
    ids, gates = expert_ids[:, 0], gate_probs[:, 0]
    weights = jnp.where(ids[..., 0:1] == expert_of, gates[..., 0:1], 0.0) + jnp.where(
        ids[..., 1:2] == expert_of, gates[..., 1:2], 0.0
    )
    weights = jnp.where(task_ids[None, :, :, None] == task_of, weights, 0.0)
    weights_items = weights.reshape(items, rows, wide)

    filled, slots, normed, inv_items, normed_quarter, weights_items = lax.optimization_barrier(
        (filled, slots, normed, inv_items, normed_quarter, weights_items)
    )
    adapters = filled.reshape(ranks, quarters, blocks, 2, combos, width)
    adapters = [adapters, adapters[:, :, 1]]
    last = HOP * (2 * sections - 1) + micros - 1

    def active(tick, section):
        position = tick - HOP * (sections - 1 - section)
        if 0 <= position < micros:
            return 1
        return 0 if 0 <= position - HOP * sections < micros else None

    def low_of(block):
        return call(
            functools.partial(low_kernel, block),
            shaped(tokens, wide),
            (normed, weights_items.reshape(blocks * tokens, wide), adapters[block]),
            2 * tokens * wide * model,
            3 << 20,
        )

    def exchanged(block, *lows):
        start = 0 if block == 1 else HOP * sections
        span = slice(start, start + micros + HOP * (sections - 1))
        fresh = block == blocks - 1
        cots = [out_grad[0] if cot is None else cot for cot in incoming[span]]
        parts = call(
            functools.partial(pack_kernel, micros, sections, fresh),
            [shaped(tokens, width + (1 + len(lows)) * wide)] * quarters,
            (where, *lows, out_grad, *cots, *dus[span]),
            0,
            3 << 20,
        )
        return swapped(parts, QUARTERS)

    def partial_grads(block, mixed, lows):
        return call(
            functools.partial(grads_kernel, block, width + (2 - block) * wide),
            shaped(ranks, 2 * combos, width),
            (*mixed, *lows, *normed_quarter),
            4 * quarters * tokens * wide * width,
            5 << 20,
        )

    incoming, dus, results = [None] * HOP, [], []
    for tick in range(last + 1):
        operands = [where]
        if tick < micros:
            operands.append(out_grad)
        if tick >= HOP:
            incoming[tick], dus[-1] = lax.optimization_barrier((incoming[tick], dus[-1]))
            operands.append(incoming[tick])
        if tick < HOP * sections:
            used = [adapters[1]]
        elif tick >= HOP * (sections - 1) + micros:
            used = [adapters[0]]
        else:
            used = [adapters[1], adapters[0]]
        result, du = call(
            functools.partial(tick_kernel, tick, sections, micros),
            [shaped(rows, model), shaped(rows, wide)],
            (*operands, x_items, inv_items, weights_items, *used),
            4 * rows * wide * model,
            5 << 20,
        )
        results.append(result)
        dus.append(du)
        if tick > last - HOP:
            continue
        pairs = [
            (i, (i - 1) % sections)
            for i in range(sections)
            if active(tick, i) == 1 or (i and active(tick, i) == 0)
        ]
        arriving = lax.ppermute(result, "s", pairs)
        if tick == 1:
            low_first = low_of(1)
            arriving, low_first = lax.optimization_barrier((arriving, low_first))
        if tick == HOP + 1:
            whole, arriving = lax.optimization_barrier((adapters[0], arriving))
            adapters[0] = whole[:, :, 0]
        if tick == 2 * HOP + 2:
            low_second = low_of(0)
            arriving, low_second = lax.optimization_barrier((arriving, low_second))
        if tick == HOP * (sections - 1) + micros - 1:
            first = exchanged(1, low_first, low_second)
        if tick == HOP * (sections - 1) + micros + 1:
            early = partial_grads(1, first, first)
            arriving, _ = lax.optimization_barrier((arriving, early))
            early = lax.all_to_all(early, RANKS, 0, 0)
        incoming.append(arriving)
    mixed = exchanged(0)
    mixed[0], early = lax.optimization_barrier((mixed[0], early))
    part = partial_grads(0, mixed, first)
    part = part.reshape(lax.axis_size("x"), -1, 2 * combos, width)
    part = lax.all_to_all(part, "x", 0, 0)
    part = jnp.sum(part.astype(f32), axis=0).astype(bf16)
    part = lax.all_to_all(part, "zh", 0, 0)
    scale = 1.0 / (micros * rows * lax.axis_size(DP))
    early = from_sections((jnp.sum(early.astype(f32), axis=0) * scale).astype(bf16))

    hidden_out = jnp.stack(
        [
            lax.select_n(
                section_id,
                *[results[m + HOP * (2 * sections - 1 - s)] for s in range(sections)],
            )
            for m in range(micros)
        ]
    )
    hidden_out, part, early = lax.optimization_barrier((hidden_out, part, early))
    late = from_sections((jnp.sum(part.astype(f32), axis=0) * scale).astype(bf16))
    pre_all = task_embed[None, None, :, None, :] + slots.swapaxes(0, 1)[:, :, None, :, :]
    cond_all = jax.nn.silu(pre_all).reshape(sections * blocks * combos, cond_width)
    grads = jnp.stack([late, early]).reshape(sections * blocks, 2, combos, width)
    grad_a = grads[:, 0].reshape(-1, width)
    grad_b = grads[:, 1].reshape(-1, width)
    d_cond = jnp.einsum("nf,wf->nw", grad_a, gen_down, preferred_element_type=f32)
    d_cond = d_cond + jnp.einsum("nf,wf->nw", grad_b, gen_up, preferred_element_type=f32)
    gate = jax.nn.sigmoid(pre_all)
    d_pre = d_cond.reshape(pre_all.shape) * gate * (1.0 + pre_all * (1.0 - gate))
    own = lax.dynamic_index_in_dim(d_pre, section_id, 1, keepdims=False)
    d_slot = jnp.sum(own, axis=1).reshape(blocks * experts, cond_width)
    d_task = jnp.sum(d_pre, axis=(0, 1, 3))
    small = jnp.concatenate([d_slot, d_task])
    held = small.reshape(-1, 128)
    held = jnp.pad(held, ((0, -held.shape[0] % 8), (0, 0)))
    got = lax.all_gather(held, QUARTERS, axis=0, tiled=True)
    held = jnp.sum(got.reshape(-1, *held.shape), axis=0)
    held = jnp.broadcast_to(held[None], (ranks, *held.shape))
    held = jnp.sum(lax.all_to_all(held, RANKS, 0, 0), axis=0)
    small = held[: small.size // 128].reshape(small.shape)
    d_slot = small[: blocks * experts].reshape(blocks, 1, experts, cond_width)
    d_task = small[blocks * experts :]
    d_gen_down = jnp.einsum("nw,nf->wf", cond_all, grad_a.astype(f32), precision=high)
    d_gen_up = jnp.einsum("nw,nf->wf", cond_all, grad_b.astype(f32), precision=high)
    return (hidden_out[None], d_gen_down, d_gen_up, d_task, d_slot)


def solution(mesh):
    split = Mesh(mesh.devices.reshape(mesh.devices.shape[0], 4, 4, 2, 2), AXES)
    placed = (
        P(None, "s", None, DP, None),
        P(None, DP, None),
        P(None, "s", None, DP, None),
        P(None, "s", None, DP, None),
        P(None, DP),
        P(),
        P(None, "s", None, None),
        P(None, DP),
        P(None, DP),
    )
    return jax.shard_map(
        on_device,
        mesh=split,
        in_specs=placed,
        out_specs=(
            P("s", None, DP, None),
            P(None, DP),
            P(None, DP),
            P(),
            P(None, "s", None, None),
        ),
        check_vma=False,
    )
```

```python
import functools

import jax
import jax.numpy as jnp
from jax import lax
from jax.experimental import pallas as pl
from jax.experimental.pallas import tpu as pltpu
from jax.sharding import Mesh, PartitionSpec as P

eps = 1e-05
bf16 = jnp.bfloat16
f32 = jnp.float32

AXES = ("s", "x", "zh", "zl", "c")
DP = ("x", "zh", "zl", "c")
RANKS = ("x", "zh")
QUARTERS = ("zl", "c")
VMEM = pl.BlockSpec(memory_space=pltpu.VMEM)
SMEM = pl.BlockSpec(memory_space=pltpu.SMEM)
LAST = (((1,), (1,)), ((), ()))
FIRST = (((0,), (0,)), ((), ()))
VMEM_LIMIT = 4 * 1024 * 1024
HOP = 1


def adapter_rows(g_ref, which, q):
    part = g_ref[:, q, which]
    return part.reshape(part.shape[0] * part.shape[1], part.shape[2])


def chosen_quarter(value, index, quarters):
    width = value.shape[1] // quarters
    part = value[:, :width]
    for q in range(1, quarters):
        part = jnp.where(index == q, value[:, q * width : (q + 1) * width], part)
    return part


def prep_kernel(where_ref, x_ref, xn_ref, inv_ref, *sent):
    items, rows, _ = x_ref.shape
    for item in range(items):
        values = x_ref[item].astype(f32)
        inv = lax.rsqrt(jnp.mean(values * values, axis=1, keepdims=True) + eps)
        inv_ref[item] = jnp.broadcast_to(inv, (rows, inv_ref.shape[2]))
        normed = (values * inv).astype(bf16)
        where = slice(item * rows, (item + 1) * rows)
        xn_ref[where, :] = normed
        for d, out_ref in enumerate(sent):
            out_ref[where, :] = chosen_quarter(normed, where_ref[1] ^ d, len(sent))


def low_kernel(block, xn_ref, weights_ref, g_ref, out_ref):
    tokens, _ = out_ref.shape
    quarters, width = g_ref.shape[1], g_ref.shape[4]
    low = jnp.zeros(out_ref.shape, f32)
    for q in range(quarters):
        low += lax.dot_general(
            xn_ref[block * tokens : (block + 1) * tokens, q * width : (q + 1) * width],
            adapter_rows(g_ref, 0, q),
            LAST,
            preferred_element_type=f32,
        )
    weights = weights_ref[block * tokens : (block + 1) * tokens, :]
    out_ref[...] = (weights * low).astype(bf16)


def tick_kernel(tick, sections, micros, where_ref, *refs):
    refs = list(refs)
    section = where_ref[0]
    if tick < micros:
        grad = refs.pop(0)[tick]
        if tick >= HOP:
            cot = jnp.where(section == sections - 1, grad, refs.pop(0)[...])
        else:
            cot = grad
    else:
        cot = refs.pop(0)[...]
    x_ref, inv_ref, weights_ref = refs[:3]
    dx_ref, du_ref = refs[-2:]
    adapters = refs[3:-2]
    position = tick - HOP * (sections - 1 - section)
    second = position - HOP * sections
    first_item = micros + jnp.clip(position, 0, micros - 1)
    second_item = jnp.clip(second, 0, micros - 1)

    def layer(g_ref, item):
        quarters, width = g_ref.shape[1], g_ref.shape[4]
        back = jnp.zeros(du_ref.shape, f32)
        for q in range(quarters):
            back += lax.dot_general(
                cot[:, q * width : (q + 1) * width],
                adapter_rows(g_ref, 1, q),
                LAST,
                preferred_element_type=f32,
            )
        du = (weights_ref[item] * back).astype(bf16)
        du_ref[...] = du
        inv = inv_ref[item][:, :1]
        dxn, xf = [], []
        total = jnp.zeros((du.shape[0], 1), f32)
        for q in range(quarters):
            xf.append(x_ref[item, :, q * width : (q + 1) * width].astype(f32) * inv)
            dxn.append(jnp.dot(du, adapter_rows(g_ref, 0, q), preferred_element_type=f32))
            total += jnp.sum(dxn[q] * xf[q], axis=1, keepdims=True)
        mean = total * (1.0 / (quarters * width))
        for q in range(quarters):
            cols = slice(q * width, (q + 1) * width)
            dx_ref[:, cols] = (
                cot[:, cols].astype(f32) + inv * (dxn[q] - xf[q] * mean)
            ).astype(bf16)

    if tick < HOP * sections:
        layer(adapters[0], first_item)
    elif tick >= HOP * (sections - 1) + micros:
        layer(adapters[0], second_item)
    else:
        pl.when(second < 0)(lambda: layer(adapters[0], first_item))
        pl.when(second >= 0)(lambda: layer(adapters[1], second_item))


def pack_kernel(micros, sections, fresh, where_ref, *refs):
    spans = micros + HOP * (sections - 1)
    lows = refs[:2] if fresh else ()
    refs = refs[len(lows) :]
    grad_ref, cots, dus, sent = refs[0], refs[1 : 1 + spans], refs[1 + spans : 1 + 2 * spans], refs[1 + 2 * spans :]
    rows, wide = dus[0].shape
    quarters = len(sent)
    width = cots[0].shape[1] // quarters
    section = where_ref[0]
    for m in range(micros):
        cot = grad_ref[m] if fresh else cots[m][...]
        du = dus[m][...]
        for s in range(sections - 1):
            at = m + HOP * (sections - 1 - s)
            cot = jnp.where(section == s, cots[at][...], cot)
            du = jnp.where(section == s, dus[at][...], du)
        where = slice(m * rows, (m + 1) * rows)
        for d, out_ref in enumerate(sent):
            out_ref[where, :width] = chosen_quarter(cot, where_ref[1] ^ d, quarters)
            out_ref[where, width : width + wide] = du
    for out_ref in sent:
        for i, low_ref in enumerate(lows):
            out_ref[:, width + (1 + i) * wide : width + (2 + i) * wide] = low_ref[...]


def grads_kernel(block, low_at, *refs):
    out_ref = refs[-1]
    quarters = len(refs) // 3
    lows, xns = refs[quarters : 2 * quarters], refs[2 * quarters : -1]
    tokens, width = refs[0].shape[0], xns[0].shape[1]
    ranks, combos = out_ref.shape[0], out_ref.shape[1] // 2
    wide = ranks * combos
    xn = jnp.concatenate([ref[block * tokens : (block + 1) * tokens, :] for ref in xns])
    mixed = jnp.concatenate([ref[:, : width + wide] for ref in refs[:quarters]])
    dy = mixed[:, :width]
    du = mixed[:, width : width + wide]
    low = jnp.concatenate([ref[:, low_at : low_at + wide] for ref in lows])
    grad_a = lax.dot_general(du, xn, FIRST, preferred_element_type=f32)
    out_ref[:, :combos, :] = grad_a.astype(bf16).reshape(ranks, combos, width)
    grad_b = lax.dot_general(low, dy, FIRST, preferred_element_type=f32)
    out_ref[:, combos:, :] = grad_b.astype(bf16).reshape(ranks, combos, width)


def generate_kernel(task_ref, slot_ref, down_ref, up_ref, out_ref):
    blocks, _, combos, _ = out_ref.shape
    pre = jnp.concatenate(
        [
            slot_ref[j] + task_ref[t : t + 1, :]
            for j in range(blocks)
            for t in range(task_ref.shape[0])
        ]
    )
    cond = pre / (1.0 + jnp.exp(-pre))
    first = cond.astype(bf16)
    rest = cond - first.astype(f32)
    second = rest.astype(bf16)
    third = (rest - second.astype(f32)).astype(bf16)
    parts = jnp.concatenate([first, second, third])
    rows = cond.shape[0]
    for which, gen_ref in enumerate((down_ref, up_ref)):
        made = jnp.dot(parts, gen_ref[...], preferred_element_type=f32)
        made = made[:rows] + (made[rows : 2 * rows] + made[2 * rows :])
        out_ref[:, which] = made.astype(bf16).reshape(blocks, combos, -1)


def call(kernel, out_shape, operands, flops, moved):
    scalars = 1 if operands[0].dtype == jnp.int32 else 0
    return pl.pallas_call(
        kernel,
        out_shape=out_shape,
        in_specs=[SMEM] * scalars + [VMEM] * (len(operands) - scalars),
        out_specs=jax.tree.map(lambda _: VMEM, out_shape),
        compiler_params=pltpu.CompilerParams(vmem_limit_bytes=VMEM_LIMIT),
        cost_estimate=pl.CostEstimate(flops=flops, bytes_accessed=moved, transcendentals=0),
    )(*operands)


def swapped(parts, axes):
    count = lax.axis_size(axes)
    return [parts[0]] + [
        lax.ppermute(parts[d], axes, [(i, i ^ d) for i in range(count)])
        for d in range(1, count)
    ]


def from_sections(part):
    count = lax.axis_size("s")
    got = [part] + [
        lax.ppermute(part, "s", [((i + d) % count, i) for i in range(count)])
        for d in range(1, count)
    ]
    me = lax.axis_index("s")
    return jnp.stack([lax.select_n(lax.rem(i + count - me, count), *got) for i in range(count)])


def on_device(
    hidden_in, out_grad, gate_probs, expert_ids, task_ids, task_embed, slot_embed, gen_down, gen_up
):
    high = lax.Precision.HIGHEST
    sections = lax.axis_size("s")
    section_id = lax.axis_index("s")
    quarters = lax.axis_size(QUARTERS)
    ranks = lax.axis_size(RANKS)
    blocks, _, micros, rows, model = hidden_in.shape
    tasks, cond_width = task_embed.shape
    experts = slot_embed.shape[2]
    combos = tasks * experts
    width = model // quarters
    wide = ranks * combos
    items = blocks * micros
    tokens = micros * rows
    where = jnp.stack([section_id, lax.axis_index(QUARTERS)]).astype(jnp.int32)

    def shaped(*shape, dtype=bf16):
        return jax.ShapeDtypeStruct(shape, dtype)

    mine = call(
        generate_kernel,
        shaped(blocks, 2, combos, width),
        (task_embed, slot_embed[:, 0], gen_down, gen_up),
        12 * blocks * combos * cond_width * width,
        5 << 18,
    )
    filled = lax.all_gather(mine.reshape(blocks * 2 * combos, width), DP, axis=0, tiled=True)

    slots = from_sections(slot_embed[:, 0])
    x_items = hidden_in[:, 0].reshape(items, rows, model)
    normed, inv_items, *sent = call(
        prep_kernel,
        [shaped(items * rows, model), shaped(items, rows, 128, dtype=f32)]
        + [shaped(items * rows, width)] * quarters,
        (where, x_items),
        8 * items * rows * model,
        3 << 20,
    )
    normed_quarter = swapped(sent, QUARTERS)
    lane = jnp.arange(wide, dtype=jnp.int32)
    expert_of, task_of = lane % experts, (lane // experts) % tasks
    ids, gates = expert_ids[:, 0], gate_probs[:, 0]
    weights = jnp.where(ids[..., 0:1] == expert_of, gates[..., 0:1], 0.0) + jnp.where(
        ids[..., 1:2] == expert_of, gates[..., 1:2], 0.0
    )
    weights = jnp.where(task_ids[None, :, :, None] == task_of, weights, 0.0)
    weights_items = weights.reshape(items, rows, wide)

    filled, slots, normed, inv_items, normed_quarter, weights_items = lax.optimization_barrier(
        (filled, slots, normed, inv_items, normed_quarter, weights_items)
    )
    adapters = filled.reshape(ranks, quarters, blocks, 2, combos, width)
    adapters = [adapters, adapters[:, :, 1]]
    last = HOP * (2 * sections - 1) + micros - 1

    def active(tick, section):
        position = tick - HOP * (sections - 1 - section)
        if 0 <= position < micros:
            return 1
        return 0 if 0 <= position - HOP * sections < micros else None

    def low_of(block):
        return call(
            functools.partial(low_kernel, block),
            shaped(tokens, wide),
            (normed, weights_items.reshape(blocks * tokens, wide), adapters[block]),
            2 * tokens * wide * model,
            3 << 20,
        )

    def exchanged(block, *lows):
        start = 0 if block == 1 else HOP * sections
        span = slice(start, start + micros + HOP * (sections - 1))
        fresh = block == blocks - 1
        cots = [out_grad[0] if cot is None else cot for cot in incoming[span]]
        parts = call(
            functools.partial(pack_kernel, micros, sections, fresh),
            [shaped(tokens, width + (1 + len(lows)) * wide)] * quarters,
            (where, *lows, out_grad, *cots, *dus[span]),
            0,
            3 << 20,
        )
        return swapped(parts, QUARTERS)

    def partial_grads(block, mixed, lows):
        return call(
            functools.partial(grads_kernel, block, width + (2 - block) * wide),
            shaped(ranks, 2 * combos, width),
            (*mixed, *lows, *normed_quarter),
            4 * quarters * tokens * wide * width,
            5 << 20,
        )

    incoming, dus, results = [None] * HOP, [], []
    for tick in range(last + 1):
        operands = [where]
        if tick < micros:
            operands.append(out_grad)
        if tick >= HOP:
            incoming[tick], dus[-1] = lax.optimization_barrier((incoming[tick], dus[-1]))
            operands.append(incoming[tick])
        if tick < HOP * sections:
            used = [adapters[1]]
        elif tick >= HOP * (sections - 1) + micros:
            used = [adapters[0]]
        else:
            used = [adapters[1], adapters[0]]
        result, du = call(
            functools.partial(tick_kernel, tick, sections, micros),
            [shaped(rows, model), shaped(rows, wide)],
            (*operands, x_items, inv_items, weights_items, *used),
            4 * rows * wide * model,
            5 << 20,
        )
        results.append(result)
        dus.append(du)
        if tick > last - HOP:
            continue
        pairs = [
            (i, (i - 1) % sections)
            for i in range(sections)
            if active(tick, i) == 1 or (i and active(tick, i) == 0)
        ]
        arriving = lax.ppermute(result, "s", pairs)
        if tick == 1:
            low_first = low_of(1)
            arriving, low_first = lax.optimization_barrier((arriving, low_first))
        if tick == HOP + 1:
            whole, arriving = lax.optimization_barrier((adapters[0], arriving))
            adapters[0] = whole[:, :, 0]
        if tick == 2 * HOP + 2:
            low_second = low_of(0)
            arriving, low_second = lax.optimization_barrier((arriving, low_second))
        if tick == HOP * (sections - 1) + micros - 1:
            arriving, dus[-1] = lax.optimization_barrier((arriving, dus[-1]))
            first = exchanged(1, low_first, low_second)
        if tick == HOP * (sections - 1) + micros:
            early = partial_grads(1, first, first)
            arriving, early = lax.optimization_barrier((arriving, early))
            early = lax.all_to_all(early, RANKS, 0, 0)
        incoming.append(arriving)
    mixed = exchanged(0)
    mixed[0], early = lax.optimization_barrier((mixed[0], early))
    part = partial_grads(0, mixed, first)
    part = part.reshape(lax.axis_size("x"), -1, 2 * combos, width)
    part = lax.all_to_all(part, "x", 0, 0)
    part = jnp.sum(part.astype(f32), axis=0).astype(bf16)
    part = lax.all_to_all(part, "zh", 0, 0)
    scale = 1.0 / (micros * rows * lax.axis_size(DP))
    early = from_sections((jnp.sum(early.astype(f32), axis=0) * scale).astype(bf16))

    hidden_out = jnp.stack(
        [
            lax.select_n(
                section_id,
                *[results[m + HOP * (2 * sections - 1 - s)] for s in range(sections)],
            )
            for m in range(micros)
        ]
    )
    hidden_out, part, early = lax.optimization_barrier((hidden_out, part, early))
    late = from_sections((jnp.sum(part.astype(f32), axis=0) * scale).astype(bf16))
    pre_all = task_embed[None, None, :, None, :] + slots.swapaxes(0, 1)[:, :, None, :, :]
    cond_all = jax.nn.silu(pre_all).reshape(sections * blocks * combos, cond_width)
    grads = jnp.stack([late, early]).reshape(sections * blocks, 2, combos, width)
    grad_a = grads[:, 0].reshape(-1, width)
    grad_b = grads[:, 1].reshape(-1, width)
    d_cond = jnp.einsum("nf,wf->nw", grad_a, gen_down, preferred_element_type=f32)
    d_cond = d_cond + jnp.einsum("nf,wf->nw", grad_b, gen_up, preferred_element_type=f32)
    gate = jax.nn.sigmoid(pre_all)
    d_pre = d_cond.reshape(pre_all.shape) * gate * (1.0 + pre_all * (1.0 - gate))
    own = lax.dynamic_index_in_dim(d_pre, section_id, 1, keepdims=False)
    d_slot = jnp.sum(own, axis=1).reshape(blocks * experts, cond_width)
    d_task = jnp.sum(d_pre, axis=(0, 1, 3))
    small = jnp.concatenate([d_slot, d_task])
    held = small.reshape(-1, 128)
    held = jnp.pad(held, ((0, -held.shape[0] % 8), (0, 0)))
    got = lax.all_gather(held, QUARTERS, axis=0, tiled=True)
    held = jnp.sum(got.reshape(-1, *held.shape), axis=0)
    held = jnp.broadcast_to(held[None], (ranks, *held.shape))
    held = jnp.sum(lax.all_to_all(held, RANKS, 0, 0), axis=0)
    small = held[: small.size // 128].reshape(small.shape)
    d_slot = small[: blocks * experts].reshape(blocks, 1, experts, cond_width)
    d_task = small[blocks * experts :]
    d_gen_down = jnp.einsum("nw,nf->wf", cond_all, grad_a.astype(f32), precision=high)
    d_gen_up = jnp.einsum("nw,nf->wf", cond_all, grad_b.astype(f32), precision=high)
    return (hidden_out[None], d_gen_down, d_gen_up, d_task, d_slot)


def solution(mesh):
    split = Mesh(mesh.devices.reshape(mesh.devices.shape[0], 4, 4, 2, 2), AXES)
    placed = (
        P(None, "s", None, DP, None),
        P(None, DP, None),
        P(None, "s", None, DP, None),
        P(None, "s", None, DP, None),
        P(None, DP),
        P(),
        P(None, "s", None, None),
        P(None, DP),
        P(None, DP),
    )
    return jax.shard_map(
        on_device,
        mesh=split,
        in_specs=placed,
        out_specs=(
            P("s", None, DP, None),
            P(None, DP),
            P(None, DP),
            P(),
            P(None, "s", None, None),
        ),
        check_vma=False,
    )
```

```python
import functools

import jax
import jax.numpy as jnp
from jax import lax
from jax.experimental import pallas as pl
from jax.experimental.pallas import tpu as pltpu
from jax.sharding import Mesh, PartitionSpec as P

eps = 1e-05
bf16 = jnp.bfloat16
f32 = jnp.float32

AXES = ("s", "x", "zh", "zl", "c")
DP = ("x", "zh", "zl", "c")
RANKS = ("x", "zh")
QUARTERS = ("zl", "c")
VMEM = pl.BlockSpec(memory_space=pltpu.VMEM)
SMEM = pl.BlockSpec(memory_space=pltpu.SMEM)
LAST = (((1,), (1,)), ((), ()))
FIRST = (((0,), (0,)), ((), ()))
VMEM_LIMIT = 4 * 1024 * 1024
HOP = 1


def adapter_rows(g_ref, which, q):
    part = g_ref[:, q, which]
    return part.reshape(part.shape[0] * part.shape[1], part.shape[2])


def chosen_quarter(value, index, quarters):
    width = value.shape[1] // quarters
    part = value[:, :width]
    for q in range(1, quarters):
        part = jnp.where(index == q, value[:, q * width : (q + 1) * width], part)
    return part


def prep_kernel(where_ref, x_ref, xn_ref, inv_ref, *sent):
    items, rows, _ = x_ref.shape
    for item in range(items):
        values = x_ref[item].astype(f32)
        inv = lax.rsqrt(jnp.mean(values * values, axis=1, keepdims=True) + eps)
        inv_ref[item] = jnp.broadcast_to(inv, (rows, inv_ref.shape[2]))
        normed = (values * inv).astype(bf16)
        where = slice(item * rows, (item + 1) * rows)
        xn_ref[where, :] = normed
        for d, out_ref in enumerate(sent):
            out_ref[where, :] = chosen_quarter(normed, where_ref[1] ^ d, len(sent))


def low_kernel(block, xn_ref, weights_ref, g_ref, out_ref):
    tokens, _ = out_ref.shape
    quarters, width = g_ref.shape[1], g_ref.shape[4]
    low = jnp.zeros(out_ref.shape, f32)
    for q in range(quarters):
        low += lax.dot_general(
            xn_ref[block * tokens : (block + 1) * tokens, q * width : (q + 1) * width],
            adapter_rows(g_ref, 0, q),
            LAST,
            preferred_element_type=f32,
        )
    weights = weights_ref[block * tokens : (block + 1) * tokens, :]
    out_ref[...] = (weights * low).astype(bf16)


def tick_kernel(tick, sections, micros, where_ref, *refs):
    refs = list(refs)
    section = where_ref[0]
    if tick < micros:
        grad = refs.pop(0)[tick]
        if tick >= HOP:
            cot = jnp.where(section == sections - 1, grad, refs.pop(0)[...])
        else:
            cot = grad
    else:
        cot = refs.pop(0)[...]
    x_ref, inv_ref, weights_ref = refs[:3]
    dx_ref, du_ref = refs[-2:]
    adapters = refs[3:-2]
    position = tick - HOP * (sections - 1 - section)
    second = position - HOP * sections
    first_item = micros + jnp.clip(position, 0, micros - 1)
    second_item = jnp.clip(second, 0, micros - 1)

    def layer(g_ref, item):
        quarters, width = g_ref.shape[1], g_ref.shape[4]
        back = jnp.zeros(du_ref.shape, f32)
        for q in range(quarters):
            back += lax.dot_general(
                cot[:, q * width : (q + 1) * width],
                adapter_rows(g_ref, 1, q),
                LAST,
                preferred_element_type=f32,
            )
        du = (weights_ref[item] * back).astype(bf16)
        du_ref[...] = du
        inv = inv_ref[item][:, :1]
        dxn, xf = [], []
        total = jnp.zeros((du.shape[0], 1), f32)
        for q in range(quarters):
            xf.append(x_ref[item, :, q * width : (q + 1) * width].astype(f32) * inv)
            dxn.append(jnp.dot(du, adapter_rows(g_ref, 0, q), preferred_element_type=f32))
            total += jnp.sum(dxn[q] * xf[q], axis=1, keepdims=True)
        mean = total * (1.0 / (quarters * width))
        for q in range(quarters):
            cols = slice(q * width, (q + 1) * width)
            dx_ref[:, cols] = (
                cot[:, cols].astype(f32) + inv * (dxn[q] - xf[q] * mean)
            ).astype(bf16)

    if tick < HOP * sections:
        layer(adapters[0], first_item)
    elif tick >= HOP * (sections - 1) + micros:
        layer(adapters[0], second_item)
    else:
        pl.when(second < 0)(lambda: layer(adapters[0], first_item))
        pl.when(second >= 0)(lambda: layer(adapters[1], second_item))


def pack_kernel(micros, sections, fresh, where_ref, *refs):
    spans = micros + HOP * (sections - 1)
    lows = refs[:2] if fresh else ()
    refs = refs[len(lows) :]
    grad_ref, cots, dus, sent = refs[0], refs[1 : 1 + spans], refs[1 + spans : 1 + 2 * spans], refs[1 + 2 * spans :]
    rows, wide = dus[0].shape
    quarters = len(sent)
    width = cots[0].shape[1] // quarters
    section = where_ref[0]
    for m in range(micros):
        cot = grad_ref[m] if fresh else cots[m][...]
        du = dus[m][...]
        for s in range(sections - 1):
            at = m + HOP * (sections - 1 - s)
            cot = jnp.where(section == s, cots[at][...], cot)
            du = jnp.where(section == s, dus[at][...], du)
        where = slice(m * rows, (m + 1) * rows)
        for d, out_ref in enumerate(sent):
            out_ref[where, :width] = chosen_quarter(cot, where_ref[1] ^ d, quarters)
            out_ref[where, width : width + wide] = du
    for out_ref in sent:
        for i, low_ref in enumerate(lows):
            out_ref[:, width + (1 + i) * wide : width + (2 + i) * wide] = low_ref[...]


def grads_kernel(block, low_at, *refs):
    out_ref = refs[-1]
    quarters = len(refs) // 3
    lows, xns = refs[quarters : 2 * quarters], refs[2 * quarters : -1]
    tokens, width = refs[0].shape[0], xns[0].shape[1]
    ranks, combos = out_ref.shape[0], out_ref.shape[1] // 2
    wide = ranks * combos
    xn = jnp.concatenate([ref[block * tokens : (block + 1) * tokens, :] for ref in xns])
    mixed = jnp.concatenate([ref[:, : width + wide] for ref in refs[:quarters]])
    dy = mixed[:, :width]
    du = mixed[:, width : width + wide]
    low = jnp.concatenate([ref[:, low_at : low_at + wide] for ref in lows])
    grad_a = lax.dot_general(du, xn, FIRST, preferred_element_type=f32)
    out_ref[:, :combos, :] = grad_a.astype(bf16).reshape(ranks, combos, width)
    grad_b = lax.dot_general(low, dy, FIRST, preferred_element_type=f32)
    out_ref[:, combos:, :] = grad_b.astype(bf16).reshape(ranks, combos, width)


def generate_kernel(task_ref, slot_ref, down_ref, up_ref, out_ref):
    blocks, _, combos, _ = out_ref.shape
    pre = jnp.concatenate(
        [
            slot_ref[j] + task_ref[t : t + 1, :]
            for j in range(blocks)
            for t in range(task_ref.shape[0])
        ]
    )
    cond = pre / (1.0 + jnp.exp(-pre))
    first = cond.astype(bf16)
    rest = cond - first.astype(f32)
    second = rest.astype(bf16)
    third = (rest - second.astype(f32)).astype(bf16)
    parts = jnp.concatenate([first, second, third])
    rows = cond.shape[0]
    for which, gen_ref in enumerate((down_ref, up_ref)):
        made = jnp.dot(parts, gen_ref[...], preferred_element_type=f32)
        made = made[:rows] + (made[rows : 2 * rows] + made[2 * rows :])
        out_ref[:, which] = made.astype(bf16).reshape(blocks, combos, -1)


def call(kernel, out_shape, operands, flops, moved):
    scalars = 1 if operands[0].dtype == jnp.int32 else 0
    return pl.pallas_call(
        kernel,
        out_shape=out_shape,
        in_specs=[SMEM] * scalars + [VMEM] * (len(operands) - scalars),
        out_specs=jax.tree.map(lambda _: VMEM, out_shape),
        compiler_params=pltpu.CompilerParams(vmem_limit_bytes=VMEM_LIMIT),
        cost_estimate=pl.CostEstimate(flops=flops, bytes_accessed=moved, transcendentals=0),
    )(*operands)


def swapped(parts, axes):
    count = lax.axis_size(axes)
    return [parts[0]] + [
        lax.ppermute(parts[d], axes, [(i, i ^ d) for i in range(count)])
        for d in range(1, count)
    ]


def from_sections(part):
    count = lax.axis_size("s")
    got = [part] + [
        lax.ppermute(part, "s", [((i + d) % count, i) for i in range(count)])
        for d in range(1, count)
    ]
    me = lax.axis_index("s")
    return jnp.stack([lax.select_n(lax.rem(i + count - me, count), *got) for i in range(count)])


def on_device(
    hidden_in, out_grad, gate_probs, expert_ids, task_ids, task_embed, slot_embed, gen_down, gen_up
):
    high = lax.Precision.HIGHEST
    sections = lax.axis_size("s")
    section_id = lax.axis_index("s")
    quarters = lax.axis_size(QUARTERS)
    ranks = lax.axis_size(RANKS)
    blocks, _, micros, rows, model = hidden_in.shape
    tasks, cond_width = task_embed.shape
    experts = slot_embed.shape[2]
    combos = tasks * experts
    width = model // quarters
    wide = ranks * combos
    items = blocks * micros
    tokens = micros * rows
    where = jnp.stack([section_id, lax.axis_index(QUARTERS)]).astype(jnp.int32)

    def shaped(*shape, dtype=bf16):
        return jax.ShapeDtypeStruct(shape, dtype)

    mine = call(
        generate_kernel,
        shaped(blocks, 2, combos, width),
        (task_embed, slot_embed[:, 0], gen_down, gen_up),
        12 * blocks * combos * cond_width * width,
        5 << 18,
    )
    filled = lax.all_gather(mine.reshape(blocks * 2 * combos, width), DP, axis=0, tiled=True)

    slots = from_sections(slot_embed[:, 0])
    x_items = hidden_in[:, 0].reshape(items, rows, model)
    normed, inv_items, *sent = call(
        prep_kernel,
        [shaped(items * rows, model), shaped(items, rows, 128, dtype=f32)]
        + [shaped(items * rows, width)] * quarters,
        (where, x_items),
        8 * items * rows * model,
        3 << 20,
    )
    normed_quarter = swapped(sent, QUARTERS)
    lane = jnp.arange(wide, dtype=jnp.int32)
    expert_of, task_of = lane % experts, (lane // experts) % tasks
    ids, gates = expert_ids[:, 0], gate_probs[:, 0]
    weights = jnp.where(ids[..., 0:1] == expert_of, gates[..., 0:1], 0.0) + jnp.where(
        ids[..., 1:2] == expert_of, gates[..., 1:2], 0.0
    )
    weights = jnp.where(task_ids[None, :, :, None] == task_of, weights, 0.0)
    weights_items = weights.reshape(items, rows, wide)

    filled, slots, normed, inv_items, normed_quarter, weights_items = lax.optimization_barrier(
        (filled, slots, normed, inv_items, normed_quarter, weights_items)
    )
    adapters = filled.reshape(ranks, quarters, blocks, 2, combos, width)
    adapters = [adapters, adapters[:, :, 1]]
    last = HOP * (2 * sections - 1) + micros - 1

    def active(tick, section):
        position = tick - HOP * (sections - 1 - section)
        if 0 <= position < micros:
            return 1
        return 0 if 0 <= position - HOP * sections < micros else None

    def low_of(block):
        return call(
            functools.partial(low_kernel, block),
            shaped(tokens, wide),
            (normed, weights_items.reshape(blocks * tokens, wide), adapters[block]),
            2 * tokens * wide * model,
            3 << 20,
        )

    def exchanged(block, *lows):
        start = 0 if block == 1 else HOP * sections
        span = slice(start, start + micros + HOP * (sections - 1))
        fresh = block == blocks - 1
        cots = [out_grad[0] if cot is None else cot for cot in incoming[span]]
        parts = call(
            functools.partial(pack_kernel, micros, sections, fresh),
            [shaped(tokens, width + (1 + len(lows)) * wide)] * quarters,
            (where, *lows, out_grad, *cots, *dus[span]),
            0,
            3 << 20,
        )
        return swapped(parts, QUARTERS)

    def partial_grads(block, mixed, lows):
        return call(
            functools.partial(grads_kernel, block, width + (2 - block) * wide),
            shaped(ranks, 2 * combos, width),
            (*mixed, *lows, *normed_quarter),
            4 * quarters * tokens * wide * width,
            5 << 20,
        )

    incoming, dus, results = [None] * HOP, [], []
    for tick in range(last + 1):
        operands = [where]
        if tick < micros:
            operands.append(out_grad)
        if tick >= HOP:
            incoming[tick], dus[-1] = lax.optimization_barrier((incoming[tick], dus[-1]))
            operands.append(incoming[tick])
        if tick < HOP * sections:
            used = [adapters[1]]
        elif tick >= HOP * (sections - 1) + micros:
            used = [adapters[0]]
        else:
            used = [adapters[1], adapters[0]]
        result, du = call(
            functools.partial(tick_kernel, tick, sections, micros),
            [shaped(rows, model), shaped(rows, wide)],
            (*operands, x_items, inv_items, weights_items, *used),
            4 * rows * wide * model,
            5 << 20,
        )
        results.append(result)
        dus.append(du)
        if tick > last - HOP:
            continue
        pairs = [
            (i, (i - 1) % sections)
            for i in range(sections)
            if active(tick, i) == 1 or tick >= HOP * sections + micros - 1 or (i and active(tick, i) == 0)
        ]
        arriving = lax.ppermute(result, "s", pairs)
        if tick == 1:
            low_first = low_of(1)
            arriving, low_first = lax.optimization_barrier((arriving, low_first))
        if tick == HOP + 1:
            whole, arriving = lax.optimization_barrier((adapters[0], arriving))
            adapters[0] = whole[:, :, 0]
        if tick == 2 * HOP + 2:
            low_second = low_of(0)
            arriving, low_second = lax.optimization_barrier((arriving, low_second))
        if tick == HOP * (sections - 1) + micros - 1:
            arriving, dus[-1] = lax.optimization_barrier((arriving, dus[-1]))
            first = exchanged(1, low_first, low_second)
        if tick == HOP * (sections - 1) + micros:
            early = partial_grads(1, first, first)
            arriving, early = lax.optimization_barrier((arriving, early))
            early = lax.all_to_all(early, RANKS, 0, 0)
        incoming.append(arriving)
    mixed = exchanged(0)
    mixed[0], early = lax.optimization_barrier((mixed[0], early))
    part = partial_grads(0, mixed, first)
    part = part.reshape(lax.axis_size("x"), -1, 2 * combos, width)
    part = lax.all_to_all(part, "x", 0, 0)
    part = jnp.sum(part.astype(f32), axis=0).astype(bf16)
    part = lax.all_to_all(part, "zh", 0, 0)
    scale = 1.0 / (micros * rows * lax.axis_size(DP))
    early = from_sections((jnp.sum(early.astype(f32), axis=0) * scale).astype(bf16))

    hidden_out = jnp.stack(
        [
            lax.select_n(
                section_id,
                *[results[m + HOP * (2 * sections - 1 - s)] for s in range(sections)],
            )
            for m in range(micros)
        ]
    )
    hidden_out, part, early = lax.optimization_barrier((hidden_out, part, early))
    late = from_sections((jnp.sum(part.astype(f32), axis=0) * scale).astype(bf16))
    pre_all = task_embed[None, None, :, None, :] + slots.swapaxes(0, 1)[:, :, None, :, :]
    cond_all = jax.nn.silu(pre_all).reshape(sections * blocks * combos, cond_width)
    grads = jnp.stack([late, early]).reshape(sections * blocks, 2, combos, width)
    grad_a = grads[:, 0].reshape(-1, width)
    grad_b = grads[:, 1].reshape(-1, width)
    d_cond = jnp.einsum("nf,wf->nw", grad_a, gen_down, preferred_element_type=f32)
    d_cond = d_cond + jnp.einsum("nf,wf->nw", grad_b, gen_up, preferred_element_type=f32)
    gate = jax.nn.sigmoid(pre_all)
    d_pre = d_cond.reshape(pre_all.shape) * gate * (1.0 + pre_all * (1.0 - gate))
    own = lax.dynamic_index_in_dim(d_pre, section_id, 1, keepdims=False)
    d_slot = jnp.sum(own, axis=1).reshape(blocks * experts, cond_width)
    d_task = jnp.sum(d_pre, axis=(0, 1, 3))
    small = jnp.concatenate([d_slot, d_task])
    held = small.reshape(-1, 128)
    held = jnp.pad(held, ((0, -held.shape[0] % 8), (0, 0)))
    got = lax.all_gather(held, QUARTERS, axis=0, tiled=True)
    held = jnp.sum(got.reshape(-1, *held.shape), axis=0)
    held = jnp.broadcast_to(held[None], (ranks, *held.shape))
    held = jnp.sum(lax.all_to_all(held, RANKS, 0, 0), axis=0)
    small = held[: small.size // 128].reshape(small.shape)
    d_slot = small[: blocks * experts].reshape(blocks, 1, experts, cond_width)
    d_task = small[blocks * experts :]
    d_gen_down = jnp.einsum("nw,nf->wf", cond_all, grad_a.astype(f32), precision=high)
    d_gen_up = jnp.einsum("nw,nf->wf", cond_all, grad_b.astype(f32), precision=high)
    return (hidden_out[None], d_gen_down, d_gen_up, d_task, d_slot)


def solution(mesh):
    split = Mesh(mesh.devices.reshape(mesh.devices.shape[0], 4, 4, 2, 2), AXES)
    placed = (
        P(None, "s", None, DP, None),
        P(None, DP, None),
        P(None, "s", None, DP, None),
        P(None, "s", None, DP, None),
        P(None, DP),
        P(),
        P(None, "s", None, None),
        P(None, DP),
        P(None, DP),
    )
    return jax.shard_map(
        on_device,
        mesh=split,
        in_specs=placed,
        out_specs=(
            P("s", None, DP, None),
            P(None, DP),
            P(None, DP),
            P(),
            P(None, "s", None, None),
        ),
        check_vma=False,
    )
```
